256 devices in a mesh: subset: 64 (over x, z, core), vocab: 4 (over y).
Axes of the slice: x: 4, y: 4, z: 8, core: 2. Of those that a mesh axis runs over, the one named last changes fastest.
Arguments:
- hidden: bfloat16 [32768, 2048], P('subset', 'vocab'), may hold values from -100 to 100
- proj_weight: bfloat16 [2048, 25600], P('subset', 'vocab'), may hold values from -1 to 1
- targets: int32 [32768], P('subset'), may hold values from 0 to 25599
- counts: int32 [64, 100, 512], P('subset', 'vocab'), may hold values from 1 to 127, as said below
- ranks: int32 [8], replicated, may hold values from 0 to 6399
Outputs:
- row_cross_entropy: float32 [32768], P('subset')
- resample_mean_losses: float32 [64, 100], P('subset', 'vocab')
- quantiles: float32 [8], replicated
The draws below stay inside these ranges and needn't reach their ends.
Inputs may be any that keep to these rules, and one draw needn't show every extreme that they name: For every subset and resample the counts over the 512 rows sum to 32768.
All inputs are finite; a program needn't handle non-finite values.
Results may differ from the reference program's by a relative error of at most 0.0003.
Values may be sent and summed in bfloat16 or wider, within the bound.
A program may use at most 128 MiB of HBM per device.

```python
import jax
import jax.numpy as jnp
from jax import lax

D = 2048
ROWS = 512
RESAMPLES = 100
QUANT = 8
VOCAB = 25600
SUBSETS = 64
TOKEN_ROW_COUNT = 32768


def shared_weight(key):
    values = jax.random.normal(jax.random.fold_in(key, 11), (D, VOCAB), jnp.float32) * (1.0 / D) ** 0.5
    return values.astype(jnp.bfloat16).astype(jnp.float32)


def draw_proj_weight(key, part):
    return shared_weight(key).astype(jnp.bfloat16)


def draw_hidden(key, part):
    scale_key = jax.random.fold_in(key, 31)
    noise_key = jax.random.fold_in(key, 32)
    subset_pos = (jnp.arange(TOKEN_ROW_COUNT) // ROWS).astype(jnp.float32)
    scales = 3.0 ** (subset_pos / max(SUBSETS - 1, 1)) * jax.random.uniform(scale_key, (TOKEN_ROW_COUNT,), jnp.float32, 0.7, 1.4)
    noise = jax.random.normal(noise_key, (TOKEN_ROW_COUNT, D), jnp.float32)
    values = noise * scales[:, None]
    return values.astype(jnp.bfloat16)


def draw_counts(key, part):
    row_offsets = jax.random.randint(jax.random.fold_in(key, 41), (SUBSETS, RESAMPLES, ROWS), 0, SUBSETS)
    shuffled = jax.random.permutation(jax.random.fold_in(key, 42), row_offsets, axis=2, independent=True)
    return (SUBSETS + row_offsets - shuffled).astype(jnp.int32)


def touch_ends(result, own_key, low, largest):
    dims = result.shape
    place = [jax.random.randint(jax.random.fold_in(own_key, axis), (), 0, dims[axis]) for axis in range(len(dims))]
    result = result.at[tuple(place)].set(low)
    longest = dims.index(max(dims))
    place[longest] = (place[longest] + 1) % dims[longest]
    return result.at[tuple(place)].set(largest)


def setup_inputs(seed: int = 0) -> dict:
    seeds = jax.random.split(jax.random.key(seed), 6)
    return {
        "hidden": draw_hidden(jax.random.fold_in(seeds[5], 71), 0),
        "proj_weight": draw_proj_weight(jax.random.fold_in(seeds[5], 71), 0),
        "targets": touch_ends(jax.random.randint(seeds[2], (TOKEN_ROW_COUNT,), 0, VOCAB), jax.random.fold_in(seeds[2], 1), 0, VOCAB - 1).astype(jnp.int32),
        "counts": draw_counts(jax.random.fold_in(seeds[5], 71), 0),
        "ranks": touch_ends(jax.random.randint(seeds[4], (QUANT,), 0, SUBSETS * RESAMPLES), jax.random.fold_in(seeds[4], 1), 0, (SUBSETS * RESAMPLES) - 1).astype(jnp.int32),
    }


def reference(hidden, proj_weight, targets, counts, ranks):
    def subset_loss(inputs):
        block_rows, block_targets = inputs
        logit_scores = jnp.dot(block_rows, proj_weight, preferred_element_type=jnp.float32)
        row_max = jnp.max(logit_scores, axis=1)
        row_total = jnp.sum(jnp.exp(logit_scores - row_max[:, None]), axis=1)
        picked = jnp.take_along_axis(logit_scores, block_targets[:, None].astype(jnp.int32), axis=1)[:, 0]
        return row_max + jnp.log(row_total) - picked

    stacked_values = lax.map(subset_loss, (hidden.reshape(SUBSETS, ROWS, D), targets.reshape(SUBSETS, ROWS)))
    row_cross_entropy = stacked_values.reshape(TOKEN_ROW_COUNT)
    resample_mean_losses = jnp.einsum("kjd,kd->kj", counts.astype(jnp.float32), stacked_values, precision=lax.Precision.HIGHEST) / (1.0 * TOKEN_ROW_COUNT)
    pooled = jnp.sort(resample_mean_losses.reshape(SUBSETS * RESAMPLES))
    positions = lax.iota(jnp.int32, SUBSETS * RESAMPLES)
    chosen = positions[:, None] == ranks[None, :]
    quantiles = jnp.sum(jnp.where(chosen, pooled[:, None], 0.0), axis=0)
    return row_cross_entropy, resample_mean_losses, quantiles
```

```python
import jax
import jax.numpy as jnp
from jax import lax
from jax.experimental import pallas as pl
from jax.experimental.pallas import tpu as pltpu
from jax.sharding import PartitionSpec as P

MESH = pl.DeviceIdType.MESH
NX, NY, NZ, NC = 4, 4, 8, 2
ROWS = 512
HALF = 256
QTR = 128
KB = 512
COLS = 6400
TILES = 13
WIDE = TILES * 128
STRIP = 32
RES = 25
ITEMS = 10
ZITEMS = 14
BIG = 3.0e38


def kernel(
    ranks, h_in, w_in, t_in, c_in,
    ce_out, mean_out, q_out,
    hb, wb, acc, mx, ssum, spick, smax, tsub, tbuf, cbuf, cpad, crhs, sbuf, stats, rows1, mine1, rows2, mine2,
    local_sem, xa_send, xa_recv, t_send, t_recv, h_send, h_recv, z_send, z_recv, c_send, c_recv,
    s_send, s_recv, g_send, g_recv, k_send, k_recv,
):
    sub = lax.axis_index("subset")
    y = lax.axis_index("vocab")
    x = sub // (NZ * NC)
    z = (sub // NC) % NZ
    c = sub % NC

    def at(xx, yy, zz, cc):
        return (((xx + NX) % NX) * (NZ * NC) + ((zz + NZ) % NZ) * NC + (cc + NC) % NC, (yy + NY) % NY)

    plane = [(dx, dy) for dx in range(NX) for dy in range(NY) if (dx, dy) != (0, 0)]
    line = [(dz, dc) for dz in range(NZ) for dc in range(NC) if (dz, dc) != (0, 0)]

    def remote(src, dst, ss, rs, dev):
        return pltpu.make_async_remote_copy(
            src_ref=src, dst_ref=dst, send_sem=ss, recv_sem=rs, device_id=dev, device_id_type=MESH
        )

    def local(src, dst, sem):
        return pltpu.make_async_copy(src, dst, sem)

    sends = []

    def start(copy):
        copy.start()
        sends.append(copy)

    own_h = local(h_in, hb.at[x, y], local_sem.at[0])
    own_h.start()

    def colrange(xx):
        return pl.ds(pl.multiple_of(((25 * xx) // 2) * 128, 128), WIDE)

    def strip(zz, cc):
        return pl.ds(pl.multiple_of(zz * (NC * STRIP) + cc * STRIP, STRIP), STRIP)

    own_w = local(w_in.at[:, colrange(x)], wb.at[x, strip(z, c), :], xa_recv.at[0])
    own_w.start()
    own_t = local(t_in, tbuf.at[x], t_recv.at[0])
    own_t.start()
    own_c = local(c_in.at[0], cbuf, local_sem.at[1])
    own_c.start()

    barrier = pltpu.get_barrier_semaphore()
    for dx, dy in plane:
        pl.semaphore_signal(barrier, inc=1, device_id=at(x + dx, y + dy, z, c), device_id_type=MESH)
    for dz, dc in line:
        pl.semaphore_signal(barrier, inc=1, device_id=at(x, y, z + dz, c + dc), device_id_type=MESH)
    pl.semaphore_wait(barrier, len(plane) + len(line))

    for d in (1, 3, 2):
        xx = (x + d) % NX
        start(
            remote(
                w_in.at[:, colrange(xx)], wb.at[x, strip(z, c), :],
                xa_send.at[d], xa_recv.at[(NX - d) % NX], at(xx, y, z, c),
            )
        )

    def wait_cols(q):
        off = (q - x + NX) % NX
        local(w_in.at[:, colrange(0)], wb.at[q, strip(z, c), :], xa_recv.at[off]).wait()

    def span(path, part):
        if part is None:
            return pl.ds(path * HALF, HALF)
        return pl.ds(path * HALF + part * QTR, QTR)

    def place(axis, along, cross, path, part):
        along, cross = (along + 4) % 4, (cross + 4) % 4
        xx, yy = (along, cross) if axis == 0 else (cross, along)
        return hb.at[xx, yy, span(path, part), :]

    def item(axis, d, j, me_along, cross):
        first, second = (0, 1) if axis == 0 else (1, 0)
        part = 0 if d == 1 else 1
        back = me_along - d
        if j == 0:
            return place(axis, me_along, cross, first, None)
        if j == 2:
            return place(axis, back, cross, first, part)
        if j in (1, 3, 5, 7):
            return place(axis, me_along, cross + {1: 0, 3: 1, 5: -1, 7: 2}[j], second, None)
        return place(axis, back, cross + {4: 0, 6: 1, 8: -1, 9: 2}[j], second, part)

    def links():
        for axis in (0, 1):
            for d in (1, -1):
                yield axis, d, 2 * axis + (0 if d == 1 else 1)

    def coords(axis):
        return (x, y) if axis == 0 else (y, x)

    def neighbour(axis, d):
        return at(x + d, y, z, c) if axis == 0 else at(x, y + d, z, c)

    def send_h(j):
        for axis, d, n in links():
            along, cross = coords(axis)
            dst = item(axis, d, j, along, cross)
            first, second = (0, 1) if axis == 0 else (1, 0)
            src = dst
            if j == 0:
                src = h_in.at[span(first, None), :]
            if j == 1:
                src = h_in.at[span(second, None), :]
            start(remote(src, dst, h_send.at[n, j], h_recv.at[n, j], neighbour(axis, d)))

    def wait_h(j):
        for axis, d, n in links():
            along, cross = coords(axis)
            got = item(axis, d, j, along - d, cross)
            remote(got, got, h_send.at[n, j], h_recv.at[n, j], neighbour(axis, d)).wait_recv()

    send_h(0)
    send_h(1)

    for d in (1, 2, 3):
        start(
            remote(t_in, tbuf.at[x], t_send.at[d], t_recv.at[(NX - d) % NX], at(x + d, y, z, c))
        )

    order = [y, (y + 1) % 4, (y + 3) % 4, (y + 2) % 4]

    def zitem(d, j):
        pair, i = divmod(j, 7)
        turn = 0 if d == 1 else 1
        return 2 * pair + (i + turn) % 2, i // 2

    def send_core(o, hops):
        ref = wb.at[order[o], strip((z - hops + NZ) % NZ, c), :]
        n = o * NZ + hops % NZ
        start(remote(ref, ref, c_send.at[n], c_recv.at[n], at(x, y, z, c + 1)))

    def wait_core(o):
        for hops in range(NZ):
            ref = wb.at[order[o], strip((z - hops + NZ) % NZ, (c + 1) % NC), :]
            n = o * NZ + hops
            remote(ref, ref, c_send.at[n], c_recv.at[n], at(x, y, z, c + 1)).wait_recv()

    def send_z(j):
        for i, d in enumerate((1, -1)):
            o, k = zitem(d, j)
            ref = wb.at[order[o], strip((z - d * k + NZ) % NZ, c), :]
            start(remote(ref, ref, z_send.at[i, j], z_recv.at[i, j], at(x, y, z + d, c)))

    def wait_z(j):
        for i, d in enumerate((1, -1)):
            o, k = zitem(d, j)
            ref = wb.at[order[o], strip((z - d * (k + 1) + NZ) % NZ, c), :]
            remote(ref, ref, z_send.at[i, j], z_recv.at[i, j], at(x, y, z + d, c)).wait_recv()
            send_core(o, d * (k + 1))

    def step_z(j):
        wait_z(j)
        if j + 2 < ZITEMS:
            if j + 2 == 7:
                own_cols(2)
                own_cols(3)
            send_z(j + 2)

    def own_cols(o):
        wait_cols(order[o])
        send_core(o, 0)

    own_cols(0)
    own_cols(1)
    send_z(0)
    send_z(1)

    lane = lax.broadcasted_iota(jnp.int32, (ROWS, 128), 1).astype(jnp.float32)
    odd = (x % 2).astype(jnp.float32)
    keep = 1.0 - odd
    away = odd * 1048576.0
    base = (y * COLS + ((25 * x) // 2) * 128).astype(jnp.float32)

    def prepare():
        local(t_in, tbuf.at[x], t_recv.at[0]).wait()
        for d in (1, 2, 3):
            ref = tbuf.at[(x + d) % NX]
            remote(ref, ref, t_send.at[d], t_recv.at[d], at(x + d, y, z, c)).wait_recv()
        for b in range(NX):
            t = tbuf[b].astype(jnp.float32) - base
            tsub[b] = jnp.broadcast_to(t, (128, ROWS)).T - lane
        own_c.wait()
        cpad[...] = jnp.zeros(cpad.shape, jnp.float32)
        cpad[pl.ds(0, RES), :] = cbuf[...].astype(jnp.float32)
        cs = cpad[...].astype(jnp.bfloat16)
        to = lax.broadcasted_iota(jnp.int32, (128, 32), 0)
        frm = lax.broadcasted_iota(jnp.int32, (128, 32), 1)
        for k, shift in ((0, 0), (1, RES * y)):
            move = jnp.where(to == frm + shift, 1.0, 0.0).astype(jnp.bfloat16)
            crhs[pl.ds(k * 128, 128), :] = jnp.dot(
                move, cs, preferred_element_type=jnp.float32
            ).astype(jnp.bfloat16)

    def tile(b, pair, lo, width):
        ka, kb = order[2 * pair], order[2 * pair + 1]
        cols = pl.ds(lo, width)
        return jnp.dot(hb[b, ka], wb[ka, :, cols], preferred_element_type=jnp.float32) + jnp.dot(
            hb[b, kb], wb[kb, :, cols], preferred_element_type=jnp.float32
        )

    def unit(b, pair):
        def put(j, value):
            if pair == 0:
                acc[b, j] = value
            else:
                value = value + acc[b, j]
                acc[b, j] = value
                mx[...] = jnp.maximum(mx[...], value)

        if pair == 1:
            mx[...] = jnp.full(mx.shape, -BIG, jnp.float32)

        @pl.loop(0, TILES // 2)
        def _(n):
            part = tile(b, pair, pl.multiple_of(n * 256, 256), 256)
            put(2 * n, part[:, :128])
            put(2 * n + 1, part[:, 128:])

        put(TILES - 1, tile(b, pair, (TILES - 1) * 128, 128))

    def finish(b):
        @pl.loop(0, ROWS // 64)
        def _(r):
            rows = pl.ds(pl.multiple_of(r * 64, 64), 64)
            top = jnp.max(mx[rows, :], axis=1, keepdims=True)
            top = jnp.broadcast_to(top, (64, 128))
            want = tsub[b, rows, :]
            total = picked = None
            for j in range(TILES):
                value = acc[b, j, rows, :]
                e = jnp.exp(value - top)
                if j == 0:
                    total = e * keep
                    picked = jnp.where(want + away == 0.0, value, 0.0)
                else:
                    total = total + e
                    picked = jnp.where(want == j * 128.0, value, picked)
            smax[rows, :] = top
            ssum[rows, :] = total
            spick[rows, :] = picked

        sbuf[b, pl.ds(0, 1), :] = smax[...].T[:1]
        sbuf[b, pl.ds(1, 1), :] = jnp.sum(ssum[...].T, axis=0, keepdims=True)
        sbuf[b, pl.ds(2, 1), :] = jnp.sum(spick[...].T, axis=0, keepdims=True)
        sbuf[b, pl.ds(3, 1), :] = jnp.zeros((1, ROWS), jnp.float32)

    def send_stats(dx):
        b = (x + dx) % NX
        for dy in range(NY):
            src, dst = sbuf.at[b], stats.at[((NX - dx) % NX) * NY + (NY - dy) % NY]
            n = dx * NY + dy
            if n == 0:
                local(src, dst, s_recv.at[0]).start()
            else:
                m = ((NX - dx) % NX) * NY + (NY - dy) % NY
                start(remote(src, dst, s_send.at[n], s_recv.at[m], at(b, y + dy, z, c)))

    def block(dx):
        return (x + dx) % NX

    wait_h(0)
    send_h(2)
    send_h(3)
    step_z(0)
    step_z(1)
    prepare()
    step_z(2)
    wait_h(1)
    send_h(4)
    step_z(3)
    wait_h(2)
    send_h(5)
    step_z(4)
    step_z(5)
    step_z(6)
    own_h.wait()
    wait_core(0)
    wait_core(1)
    unit(block(0), 0)
    wait_h(3)
    send_h(6)
    step_z(7)
    unit(block(1), 0)
    wait_h(4)
    send_h(7)
    step_z(8)
    step_z(9)
    wait_h(5)
    send_h(8)
    step_z(10)
    unit(block(3), 0)
    step_z(11)
    wait_h(6)
    step_z(12)
    step_z(13)
    wait_core(2)
    wait_core(3)
    unit(block(0), 1)
    finish(block(0))
    send_stats(0)
    wait_h(7)
    send_h(9)
    unit(block(2), 0)
    unit(block(1), 1)
    finish(block(1))
    send_stats(1)
    wait_h(8)
    unit(block(3), 1)
    finish(block(3))
    send_stats(3)
    wait_h(9)
    unit(block(2), 1)
    finish(block(2))
    send_stats(2)

    local(sbuf.at[x], stats.at[0], s_recv.at[0]).wait()
    for n in range(1, NX * NY):
        ref = stats.at[n]
        remote(ref, ref, s_send.at[n], s_recv.at[n], at(x, y, z, c)).wait_recv()
    tops = [stats[n, 0:1, :] for n in range(NX * NY)]
    top = tops[0]
    for t in tops[1:]:
        top = jnp.maximum(top, t)
    total = jnp.zeros((1, ROWS), jnp.float32)
    target = jnp.zeros((1, ROWS), jnp.float32)
    for n in range(NX * NY):
        total = total + stats[n, 1:2, :] * jnp.exp(tops[n] - top)
        target = target + stats[n, 2:3, :]
    ce = top + jnp.log(total) - target
    ce_out[...] = ce

    high = ce.astype(jnp.bfloat16)
    rest = ce - high.astype(jnp.float32)
    middle = rest.astype(jnp.bfloat16)
    low = (rest - middle.astype(jnp.float32)).astype(jnp.bfloat16)
    which = lax.broadcasted_iota(jnp.int32, (16, ROWS), 0)
    pieces = jnp.where(
        which == 0,
        high.astype(jnp.float32),
        jnp.where(which == 1, middle.astype(jnp.float32), jnp.where(which == 2, low.astype(jnp.float32), 0.0)),
    ).astype(jnp.bfloat16)
    sums = lax.dot_general(
        pieces, crhs[...], (((1,), (1,)), ((), ())), preferred_element_type=jnp.float32
    )
    means = jnp.sum(sums, axis=0, keepdims=True) * (1.0 / 32768.0)
    mean_out[...] = means[:, :RES]
    mine1[...] = means[:, 128:]

    for dx, dy in plane:
        n = dx * NY + dy
        m = ((NX - dx) % NX) * NY + (NY - dy) % NY
        start(remote(mine1, rows1.at[m], g_send.at[n], g_recv.at[m], at(x + dx, y + dy, z, c)))
    for dx, dy in plane:
        n = dx * NY + dy
        ref = rows1.at[n]
        remote(ref, ref, g_send.at[n], g_recv.at[n], at(x, y, z, c)).wait_recv()
    for dx in range(NX):
        line_sum = mine1[...] if dx == 0 else rows1[dx * NY]
        for dy in range(1, NY):
            line_sum = line_sum + rows1[dx * NY + dy]
        mine2[pl.ds(dx, 1), :] = line_sum
    for dz, dc in line:
        n = dz * NC + dc
        m = ((NZ - dz) % NZ) * NC + dc
        start(remote(mine2, rows2.at[m], k_send.at[n], k_recv.at[m], at(x, y, z + dz, c + dc)))
    rows2[0] = mine2[...]
    for dz, dc in line:
        n = dz * NC + dc
        ref = rows2.at[n]
        remote(ref, ref, k_send.at[n], k_recv.at[n], at(x, y, z, c)).wait_recv()

    col = lax.broadcasted_iota(jnp.int32, (8, 128), 1)
    rowi = lax.broadcasted_iota(jnp.int32, (8, 128), 0)
    want = jnp.zeros((8, 128), jnp.float32)
    for q in range(8):
        want = jnp.where(rowi == q, ranks[q].astype(jnp.float32), want)
    out_of = col >= NY * RES

    def below(cands):
        counts = [jnp.zeros((8, 128), jnp.float32) for _ in cands]
        for n in range(NZ * NC):
            for r in range(NX):
                v = jnp.broadcast_to(rows2[n, pl.ds(r, 1), :], (8, 128))
                v = jnp.where(out_of, BIG, v)
                counts = [k + jnp.where(v < t, 1.0, 0.0) for k, t in zip(counts, cands)]
        return [jnp.broadcast_to(jnp.sum(k, axis=1, keepdims=True), (8, 128)) for k in counts]

    def pick(lo, cands):
        for k, t in zip(below(cands), cands):
            lo = jnp.where(k <= want, t, lo)
        return lo

    tiny = 2.0**-126
    lo = jnp.full((8, 128), tiny, jnp.float32)
    for e in (64, 16, 4, 1):
        first = lo * 2.0**e
        lo = pick(lo, [first, first * 2.0**e, first * 2.0**e * 2.0**e])
    unit0 = lo

    def refine(_, carry):
        lo, part = carry
        quarter = part * 0.25
        return pick(lo, [lo + quarter, lo + 2.0 * quarter, lo + 3.0 * quarter]), quarter

    lo, part = lax.fori_loop(0, 11, refine, (lo, unit0))
    lo = pick(lo, [lo + part * 0.5])
    none = below([jnp.full((8, 128), tiny, jnp.float32)])[0] > want
    lo = jnp.where(none, 0.0, lo)
    q_out[...] = jnp.sum(jnp.where(col == rowi, lo, 0.0), axis=0, keepdims=True)[:, :8]

    for copy in sends:
        copy.wait_send()


def shards(hidden, proj_weight, targets, counts, ranks):
    f32, bf16, i32 = jnp.float32, jnp.bfloat16, jnp.int32
    dma = pltpu.SemaphoreType.DMA
    hbm = pl.BlockSpec(memory_space=pl.ANY)
    vmem = pl.BlockSpec(memory_space=pltpu.VMEM)
    ce, means, quantiles = pl.pallas_call(
        kernel,
        out_shape=(
            jax.ShapeDtypeStruct((1, ROWS), f32),
            jax.ShapeDtypeStruct((1, RES), f32),
            jax.ShapeDtypeStruct((1, 8), f32),
        ),
        in_specs=[pl.BlockSpec(memory_space=pltpu.SMEM), hbm, hbm, hbm, hbm],
        out_specs=(vmem, vmem, vmem),
        scratch_shapes=[
            pltpu.VMEM((NX, NY, ROWS, KB), bf16),
            pltpu.VMEM((4, KB, WIDE), bf16),
            pltpu.VMEM((NX, TILES, ROWS, 128), f32),
            pltpu.VMEM((ROWS, 128), f32),
            pltpu.VMEM((ROWS, 128), f32),
            pltpu.VMEM((ROWS, 128), f32),
            pltpu.VMEM((ROWS, 128), f32),
            pltpu.VMEM((NX, ROWS, 128), f32),
            pltpu.VMEM((NX, 1, ROWS), i32),
            pltpu.VMEM((RES, ROWS), i32),
            pltpu.VMEM((32, ROWS), f32),
            pltpu.VMEM((256, ROWS), bf16),
            pltpu.VMEM((NX, 4, ROWS), f32),
            pltpu.VMEM((NX * NY, 4, ROWS), f32),
            pltpu.VMEM((NX * NY, 1, 128), f32),
            pltpu.VMEM((1, 128), f32),
            pltpu.VMEM((NZ * NC, NX, 128), f32),
            pltpu.VMEM((NX, 128), f32),
            dma((2,)),
            dma((4,)), dma((4,)),
            dma((4,)), dma((4,)),
            dma((4, ITEMS)), dma((4, ITEMS)),
            dma((2, ZITEMS)), dma((2, ZITEMS)),
            dma((4 * NZ,)), dma((4 * NZ,)),
            dma((16,)), dma((16,)),
            dma((16,)), dma((16,)),
            dma((16,)), dma((16,)),
        ],
        compiler_params=pltpu.CompilerParams(
            collective_id=0, has_side_effects=True, vmem_limit_bytes=60 * 2**20
        ),
    )(ranks, hidden, proj_weight, targets.reshape(1, ROWS), counts)
    return ce.reshape(ROWS), means, quantiles.reshape(8)


def solution(mesh):
    return jax.shard_map(
        shards,
        mesh=mesh,
        in_specs=(
            P("subset", "vocab"),
            P("subset", "vocab"),
            P("subset"),
            P("subset", "vocab", None),
            P(),
        ),
        out_specs=(P("subset"), P("subset", "vocab"), P()),
        check_vma=False,
    )
```

```python
import jax
import jax.numpy as jnp
from jax import lax
from jax.experimental import pallas as pl
from jax.experimental.pallas import tpu as pltpu
from jax.sharding import PartitionSpec as P

MESH = pl.DeviceIdType.MESH
NX, NY, NZ, NC = 4, 4, 8, 2
ROWS = 512
HALF = 256
QTR = 128
KB = 512
COLS = 6400
TILES = 13
WIDE = TILES * 128
STRIP = 16
RES = 25
ITEMS = 10
ZITEMS = 28
BIG = 3.0e38


def kernel(
    ranks, h_in, w_in, t_in, c_in,
    ce_out, mean_out, q_out,
    hb, wb, acc, apack, tsub, tbuf, cbuf, cpad, call, sbuf, stats_x, joined, stats_y, rows1, mine1, rows2, mine2,
    local_sem, xa_send, xa_recv, t_send, t_recv, h_send, h_recv, z_send, z_recv, c_send, c_recv,
    n_send, n_recv, s_send, s_recv, y_send, y_recv, g_send, g_recv, k_send, k_recv,
):
    sub = lax.axis_index("subset")
    y = lax.axis_index("vocab")
    x = sub // (NZ * NC)
    z = (sub // NC) % NZ
    c = sub % NC

    def at(xx, yy, zz, cc):
        return (((xx + NX) % NX) * (NZ * NC) + ((zz + NZ) % NZ) * NC + (cc + NC) % NC, (yy + NY) % NY)

    def remote(src, dst, ss, rs, dev):
        return pltpu.make_async_remote_copy(
            src_ref=src, dst_ref=dst, send_sem=ss, recv_sem=rs, device_id=dev, device_id_type=MESH
        )

    def local(src, dst, sem):
        return pltpu.make_async_copy(src, dst, sem)

    sends = []

    def start(copy):
        copy.start()
        sends.append(copy)

    def drain():
        for copy in sends:
            copy.wait_send()
        sends.clear()

    barrier = pltpu.get_barrier_semaphore()
    friends = [
        at(x + 1, y, z, c), at(x + 2, y, z, c), at(x + 3, y, z, c), at(x, y + 1, z, c), at(x, y + 3, z, c),
        at(x, y, z + 1, c), at(x, y, z - 1, c), at(x, y, z, c + 1),
    ]
    for friend in friends:
        pl.semaphore_signal(barrier, inc=1, device_id=friend, device_id_type=MESH)

    def colrange(xx):
        return pl.ds(pl.multiple_of(((25 * xx) // 2) * 128, 128), WIDE)

    def strip(zz, cc, half):
        start_row = zz * (NC * 2 * STRIP) + cc * (2 * STRIP)
        if half is None:
            return pl.ds(pl.multiple_of(start_row, 2 * STRIP), 2 * STRIP)
        return pl.ds(pl.multiple_of(start_row + half * STRIP, STRIP), STRIP)

    own_w = local(w_in.at[:, colrange(x)], wb.at[x, strip(z, c, None), :], xa_recv.at[0])
    own_w.start()
    own_h = local(h_in, hb.at[x, y], local_sem.at[0])
    own_h.start()
    own_t = local(t_in, tbuf.at[x], t_recv.at[0])
    own_t.start()
    own_c = local(c_in, cbuf, local_sem.at[1])
    own_c.start()
    pl.semaphore_wait(barrier, len(friends))

    for d in (1, 3, 2):
        xx = (x + d) % NX
        start(
            remote(
                w_in.at[:, colrange(xx)], wb.at[x, strip(z, c, None), :],
                xa_send.at[d], xa_recv.at[(NX - d) % NX], at(xx, y, z, c),
            )
        )

    def wait_cols(q):
        off = (q - x + NX) % NX
        local(w_in.at[:, colrange(0)], wb.at[q, strip(z, c, None), :], xa_recv.at[off]).wait()

    def span(path, part):
        if part is None:
            return pl.ds(path * HALF, HALF)
        return pl.ds(path * HALF + part * QTR, QTR)

    def place(axis, along, cross, path, part):
        along, cross = (along + 4) % 4, (cross + 4) % 4
        xx, yy = (along, cross) if axis == 0 else (cross, along)
        return hb.at[xx, yy, span(path, part), :]

    def item(axis, d, j, me_along, cross):
        first, second = (0, 1) if axis == 0 else (1, 0)
        part = 0 if d == 1 else 1
        back = me_along - d
        if j == 0:
            return place(axis, me_along, cross, first, None)
        if j == 2:
            return place(axis, back, cross, first, part)
        if j in (1, 3, 5, 7):
            return place(axis, me_along, cross + {1: 0, 3: 1, 5: -1, 7: 2}[j], second, None)
        return place(axis, back, cross + {4: 0, 6: 1, 8: -1, 9: 2}[j], second, part)

    def links():
        for axis in (0, 1):
            for d in (1, -1):
                yield axis, d, 2 * axis + (0 if d == 1 else 1)

    def coords(axis):
        return (x, y) if axis == 0 else (y, x)

    def neighbour(axis, d):
        return at(x + d, y, z, c) if axis == 0 else at(x, y + d, z, c)

    def send_h(j):
        for axis, d, n in links():
            along, cross = coords(axis)
            dst = item(axis, d, j, along, cross)
            first, second = (0, 1) if axis == 0 else (1, 0)
            src = dst
            if j == 0:
                src = h_in.at[span(first, None), :]
            if j == 1:
                src = h_in.at[span(second, None), :]
            start(remote(src, dst, h_send.at[n, j], h_recv.at[n, j], neighbour(axis, d)))

    def wait_h(j):
        for axis, d, n in links():
            along, cross = coords(axis)
            got = item(axis, d, j, along - d, cross)
            remote(got, got, h_send.at[n, j], h_recv.at[n, j], neighbour(axis, d)).wait_recv()

    send_h(0)
    send_h(1)

    for d in (1, 2, 3):
        start(
            remote(t_in, tbuf.at[x], t_send.at[d], t_recv.at[(NX - d) % NX], at(x + d, y, z, c))
        )

    order = [y, (y + 1) % 4, (y + 3) % 4, (y + 2) % 4]

    def zitem(d, j):
        quarter, i = divmod(j, 7)
        turn = 0 if d == 1 else 1
        return quarter, (i + turn) % 2, i // 2

    def send_core(o, hops):
        ref = wb.at[order[o], strip((z - hops + NZ) % NZ, c, None), :]
        n = o * NZ + hops % NZ
        start(remote(ref, ref, c_send.at[n], c_recv.at[n], at(x, y, z, c + 1)))

    def wait_core(o):
        for hops in range(NZ):
            ref = wb.at[order[o], strip((z - hops + NZ) % NZ, (c + 1) % NC, None), :]
            n = o * NZ + hops
            remote(ref, ref, c_send.at[n], c_recv.at[n], at(x, y, z, c + 1)).wait_recv()

    def send_z(j):
        for i, d in enumerate((1, -1)):
            o, half, k = zitem(d, j)
            ref = wb.at[order[o], strip((z - d * k + NZ) % NZ, c, half), :]
            start(remote(ref, ref, z_send.at[i, j], z_recv.at[i, j], at(x, y, z + d, c)))

    def own_cols(o):
        wait_cols(order[o])
        send_core(o, 0)

    def step_z(j):
        for i, d in enumerate((1, -1)):
            o, half, k = zitem(d, j)
            ref = wb.at[order[o], strip((z - d * (k + 1) + NZ) % NZ, c, half), :]
            remote(ref, ref, z_send.at[i, j], z_recv.at[i, j], at(x, y, z + d, c)).wait_recv()
        if j + 2 < ZITEMS:
            if (j + 2) % 7 == 0:
                own_cols((j + 2) // 7)
            send_z(j + 2)
        if j % 7 in (1, 3, 5):
            for d in (1, -1):
                o, half, k = zitem(d, j)
                send_core(o, d * (k + 1))
        if j % 7 == 6:
            send_core(j // 7, 4)

    own_cols(0)
    send_z(0)
    send_z(1)

    odd = (x % 2).astype(jnp.float32)
    keep = 1.0 - odd
    away = odd * 1048576.0
    base = (y * COLS + ((25 * x) // 2) * 128).astype(jnp.float32)

    def prepare():
        own_c.wait()
        cpad[...] = jnp.zeros(cpad.shape, jnp.float32)
        for i in range(RES):
            cpad[pl.ds(i, 1), :] = cbuf[i].astype(jnp.float32)
        call[y] = cpad[...].astype(jnp.bfloat16)
        for d in (1, 3, 2):
            ref = call.at[y]
            start(remote(ref, ref, n_send.at[d], n_recv.at[(NY - d) % NY], at(x, y + d, z, c)))
        own_t.wait()
        for d in (1, 2, 3):
            ref = tbuf.at[(x + d) % NX]
            remote(ref, ref, t_send.at[d], t_recv.at[d], at(x + d, y, z, c)).wait_recv()
        lane = lax.broadcasted_iota(jnp.int32, (ROWS, 128), 1).astype(jnp.float32)
        for b in range(NX):
            t = tbuf[b].astype(jnp.float32) - base
            tsub[b] = jnp.broadcast_to(t, (128, ROWS)).T - lane
        apack[...] = jnp.zeros(apack.shape, jnp.float32)

    def block(dx):
        return (x + dx) % NX

    def unit(dx, o):
        b, q = block(dx), order[o]
        part = jnp.dot(hb[b, q], wb[q], preferred_element_type=jnp.float32)
        if o == 0:
            acc[b] = part
        else:
            acc[b] += part

    def finish(dx):
        b = block(dx)

        @pl.loop(0, ROWS // 64)
        def _(r):
            rows = pl.ds(pl.multiple_of(r * 64, 64), 64)

            def piece(j):
                return acc[b, rows, pl.ds(j * 128, 128)]

            top = piece(0)
            for j in range(1, TILES):
                top = jnp.maximum(top, piece(j))
            top = jnp.broadcast_to(jnp.max(top, axis=1, keepdims=True), (64, 128))
            want = tsub[b, rows, :]
            total = jnp.exp(piece(0) - top) * keep
            picked = jnp.where(want + away == 0.0, piece(0), 0.0)
            for j in range(1, TILES):
                value = piece(j)
                total = total + jnp.exp(value - top)
                picked = jnp.where(want == j * 128.0, value, picked)
            total = jnp.sum(total, axis=1, keepdims=True)
            picked = jnp.sum(picked, axis=1, keepdims=True)
            lane = lax.broadcasted_iota(jnp.int32, (64, 128), 1)
            group = r // 2
            to = pl.ds(pl.multiple_of((r % 2) * 64, 64), 64)
            apack[to, :] = jnp.where(
                lane == group, top, jnp.where(lane == group + 4, total, jnp.where(lane == group + 8, picked, apack[to, :]))
            )

        sbuf[b] = apack[...].T[:16]
        if dx:
            m = NX - dx
            start(remote(sbuf.at[b], stats_x.at[m], s_send.at[dx], s_recv.at[m], at(b, y, z, c)))

    wait_h(0)
    send_h(2)
    send_h(3)
    step_z(0)
    step_z(1)
    prepare()
    for j in (2, 3, 4):
        step_z(j)
    wait_h(1)
    send_h(4)
    step_z(5)
    step_z(6)
    own_h.wait()
    wait_core(0)
    unit(0, 0)
    step_z(7)
    wait_h(2)
    send_h(5)
    unit(1, 0)
    step_z(8)
    unit(3, 0)
    for j in (9, 10, 11):
        step_z(j)
    wait_h(3)
    send_h(6)
    step_z(12)
    step_z(13)
    wait_core(1)
    unit(0, 1)
    step_z(14)
    wait_h(4)
    send_h(7)
    unit(1, 1)
    step_z(15)
    unit(2, 0)
    for j in (16, 17, 18):
        step_z(j)
    wait_h(5)
    send_h(8)
    step_z(19)
    step_z(20)
    unit(3, 1)
    step_z(21)
    wait_core(2)
    unit(0, 2)
    wait_h(6)
    step_z(22)
    unit(1, 2)
    step_z(23)
    unit(3, 2)
    step_z(24)
    step_z(25)
    wait_h(7)
    send_h(9)
    unit(2, 1)
    step_z(26)
    step_z(27)
    wait_core(3)
    unit(0, 3)
    finish(0)
    unit(1, 3)
    finish(1)
    wait_h(8)
    unit(2, 2)
    unit(3, 3)
    finish(3)
    wait_h(9)
    unit(2, 3)
    finish(2)

    drain()
    for d in (1, 2, 3):
        ref = call.at[(y + d) % NY]
        remote(ref, ref, n_send.at[d], n_recv.at[d], at(x, y + d, z, c)).wait_recv()

    def join(parts):
        tops = [p[0:4] for p in parts]
        top = jnp.maximum(jnp.maximum(tops[0], tops[1]), jnp.maximum(tops[2], tops[3]))
        total = parts[0][4:8] * jnp.exp(tops[0] - top)
        target = parts[0][8:12]
        for p, t in zip(parts[1:], tops[1:]):
            total = total + p[4:8] * jnp.exp(t - top)
            target = target + p[8:12]
        return top, total, target

    for d in (1, 3, 2):
        ref = stats_x.at[d]
        remote(ref, ref, s_send.at[d], s_recv.at[d], at(x + d, y, z, c)).wait_recv()
    top, total, target = join([sbuf[x], stats_x[1], stats_x[2], stats_x[3]])
    joined[pl.ds(0, 4), :] = top
    joined[pl.ds(4, 4), :] = total
    joined[pl.ds(8, 4), :] = target
    joined[pl.ds(12, 4), :] = target
    for d in (2, 1, 3):
        m = NY - d
        start(remote(joined, stats_y.at[m], y_send.at[d], y_recv.at[m], at(x, y + d, z, c)))
    for d in (1, 3, 2):
        ref = stats_y.at[d]
        remote(ref, ref, y_send.at[d], y_recv.at[d], at(x, y + d, z, c)).wait_recv()
    top, total, target = join([joined[...], stats_y[1], stats_y[2], stats_y[3]])
    ce = top + jnp.log(total) - target
    ce_out[...] = ce

    ce = jnp.concatenate([ce[g : g + 1] for g in range(4)], axis=1)
    high = ce.astype(jnp.bfloat16).astype(jnp.float32)
    middle = (ce - high).astype(jnp.bfloat16).astype(jnp.float32)
    low = (ce - high) - middle
    which = lax.broadcasted_iota(jnp.int32, (16, ROWS), 0)
    pieces = jnp.where(which == 0, high, jnp.where(which == 1, middle, jnp.where(which == 2, low, 0.0)))
    pieces = pieces.astype(jnp.bfloat16)

    def means_of(rhs):
        sums = lax.dot_general(
            pieces, rhs, (((1,), (1,)), ((), ())), preferred_element_type=jnp.float32
        )
        return jnp.sum(sums, axis=0, keepdims=True) * (1.0 / 32768.0)

    means = means_of(call[...].reshape(128, ROWS))
    lanes = lax.broadcasted_iota(jnp.int32, (1, 128), 1)
    mine1[...] = jnp.where(lanes % 32 < RES, means, BIG)

    others = [(dx, dc) for dx in range(NX) for dc in range(NC) if (dx, dc) != (0, 0)]
    for dx, dc in others:
        n, m = dx * NC + dc, ((NX - dx) % NX) * NC + dc
        start(remote(mine1, rows1.at[m], g_send.at[n], g_recv.at[m], at(x + dx, y, z, c + dc)))
    mean_out[...] = means_of(call[y])[:, :RES]
    mine2[pl.ds(0, 1), :] = mine1[...]
    for dx, dc in others:
        n = dx * NC + dc
        ref = rows1.at[n]
        remote(ref, ref, g_send.at[n], g_recv.at[n], at(x + dx, y, z, c + dc)).wait_recv()
        mine2[pl.ds(n, 1), :] = rows1[n]
    for d in (4, 3, 5, 2, 6, 1, 7):
        m = NZ - d
        start(remote(mine2, rows2.at[m], k_send.at[d], k_recv.at[m], at(x, y, z + d, c)))
    rows2[0] = mine2[...]
    for d in (1, 7, 2, 6, 3, 5, 4):
        ref = rows2.at[d]
        remote(ref, ref, k_send.at[d], k_recv.at[d], at(x, y, z + d, c)).wait_recv()

    col = lax.broadcasted_iota(jnp.int32, (8, 128), 1)
    rowi = lax.broadcasted_iota(jnp.int32, (8, 128), 0)
    want = jnp.zeros((8, 128), jnp.float32)
    for q in range(8):
        want = jnp.where(rowi == q, ranks[q].astype(jnp.float32), want)

    def below(cands):
        counts = [jnp.zeros((8, 128), jnp.float32) for _ in cands]
        for n in range(NZ):
            for r in range(8):
                v = jnp.broadcast_to(rows2[n, pl.ds(r, 1), :], (8, 128))
                counts = [k + jnp.where(v < t, 1.0, 0.0) for k, t in zip(counts, cands)]
        return [jnp.broadcast_to(jnp.sum(k, axis=1, keepdims=True), (8, 128)) for k in counts]

    def pick(lo, cands):
        for k, t in zip(below(cands), cands):
            lo = jnp.where(k <= want, t, lo)
        return lo

    tiny = 2.0**-126
    lo = jnp.full((8, 128), tiny, jnp.float32)
    for e in (64, 16, 4, 1):
        first = lo * 2.0**e
        lo = pick(lo, [first, first * 2.0**e, first * 2.0**e * 2.0**e])
    unit0 = lo

    def refine(_, carry):
        lo, part = carry
        quarter = part * 0.25
        return pick(lo, [lo + quarter, lo + 2.0 * quarter, lo + 3.0 * quarter]), quarter

    lo, part = lax.fori_loop(0, 11, refine, (lo, unit0))
    lo = pick(lo, [lo + part * 0.5])
    none = below([jnp.full((8, 128), tiny, jnp.float32)])[0] > want
    lo = jnp.where(none, 0.0, lo)
    q_out[...] = jnp.sum(jnp.where(col == rowi, lo, 0.0), axis=0, keepdims=True)[:, :8]
    drain()


def shards(hidden, proj_weight, targets, counts, ranks):
    f32, bf16, i32 = jnp.float32, jnp.bfloat16, jnp.int32
    dma = pltpu.SemaphoreType.DMA
    hbm = pl.BlockSpec(memory_space=pl.ANY)
    vmem = pl.BlockSpec(memory_space=pltpu.VMEM)
    ce, means, quantiles = pl.pallas_call(
        kernel,
        out_shape=(
            jax.ShapeDtypeStruct((4, 128), f32),
            jax.ShapeDtypeStruct((1, RES), f32),
            jax.ShapeDtypeStruct((1, 8), f32),
        ),
        in_specs=[pl.BlockSpec(memory_space=pltpu.SMEM), hbm, hbm, hbm, hbm],
        out_specs=(vmem, vmem, vmem),
        scratch_shapes=[
            pltpu.VMEM((NX, NY, ROWS, KB), bf16),
            pltpu.VMEM((4, KB, WIDE), bf16),
            pltpu.VMEM((NX, ROWS, WIDE), f32),
            pltpu.VMEM((128, 128), f32),
            pltpu.VMEM((NX, ROWS, 128), f32),
            pltpu.VMEM((NX, 1, ROWS), i32),
            pltpu.VMEM((RES, 1, ROWS), i32),
            pltpu.VMEM((32, ROWS), f32),
            pltpu.VMEM((NY, 32, ROWS), bf16),
            pltpu.VMEM((NX, 16, 128), f32),
            pltpu.VMEM((NX, 16, 128), f32),
            pltpu.VMEM((16, 128), f32),
            pltpu.VMEM((NY, 16, 128), f32),
            pltpu.VMEM((8, 1, 128), f32),
            pltpu.VMEM((1, 128), f32),
            pltpu.VMEM((NZ, 8, 128), f32),
            pltpu.VMEM((8, 128), f32),
            dma((2,)),
            dma((4,)), dma((4,)),
            dma((4,)), dma((4,)),
            dma((4, ITEMS)), dma((4, ITEMS)),
            dma((2, ZITEMS)), dma((2, ZITEMS)),
            dma((4 * NZ,)), dma((4 * NZ,)),
            dma((4,)), dma((4,)),
            dma((4,)), dma((4,)),
            dma((4,)), dma((4,)),
            dma((8,)), dma((8,)),
            dma((8,)), dma((8,)),
        ],
        compiler_params=pltpu.CompilerParams(
            collective_id=0, has_side_effects=True, vmem_limit_bytes=60 * 2**20
        ),
    )(ranks, hidden, proj_weight, targets.reshape(1, ROWS), counts.transpose(1, 0, 2))
    return ce.reshape(ROWS), means, quantiles.reshape(8)


def solution(mesh):
    return jax.shard_map(
        shards,
        mesh=mesh,
        in_specs=(
            P("subset", "vocab"),
            P("subset", "vocab"),
            P("subset"),
            P("subset", "vocab", None),
            P(),
        ),
        out_specs=(P("subset"), P("subset", "vocab"), P()),
        check_vma=False,
    )
```

```python
import jax
import jax.numpy as jnp
from jax import lax
from jax.experimental import pallas as pl
from jax.experimental.pallas import tpu as pltpu
from jax.sharding import PartitionSpec as P

MESH = pl.DeviceIdType.MESH
NX, NY, NZ, NC = 4, 4, 8, 2
ROWS = 512
SHARES = {
    (0, None): (0, 272), (0, 0): (0, 144), (0, 1): (144, 128),
    (1, None): (272, 240), (1, 0): (272, 128), (1, 1): (400, 112),
}
KB = 512
COLS = 6400
TILES = 13
WIDE = TILES * 128
STRIP = 32
RES = 25
ITEMS = 10
ZITEMS = 14
BIG = 3.0e38


def kernel(
    ranks, h_in, w_in, t_in, c_in,
    ce_out, mean_out, q_out,
    hb, wb, acc, tsub, tbuf, cbuf, cpad, call, sbuf, stats, rows1, mine1, rows2, mine2,
    local_sem, xa_send, xa_recv, t_send, t_recv, h_send, h_recv, z_send, z_recv, c_send, c_recv,
    n_send, n_recv, s_send, s_recv, g_send, g_recv, k_send, k_recv,
):
    sub = lax.axis_index("subset")
    y = lax.axis_index("vocab")
    x = sub // (NZ * NC)
    z = (sub // NC) % NZ
    c = sub % NC

    def at(xx, yy, zz, cc):
        return (((xx + NX) % NX) * (NZ * NC) + ((zz + NZ) % NZ) * NC + (cc + NC) % NC, (yy + NY) % NY)

    def remote(src, dst, ss, rs, dev):
        return pltpu.make_async_remote_copy(
            src_ref=src, dst_ref=dst, send_sem=ss, recv_sem=rs, device_id=dev, device_id_type=MESH
        )

    def local(src, dst, sem):
        return pltpu.make_async_copy(src, dst, sem)

    sends = []

    def start(copy):
        copy.start()
        sends.append(copy)

    def drain():
        for copy in sends:
            copy.wait_send()
        sends.clear()

    barrier = pltpu.get_barrier_semaphore()
    friends = [
        at(x + 1, y, z, c), at(x + 2, y, z, c), at(x + 3, y, z, c), at(x, y + 1, z, c), at(x, y + 3, z, c),
        at(x, y, z + 1, c), at(x, y, z - 1, c), at(x, y, z, c + 1),
    ]
    for friend in friends:
        pl.semaphore_signal(barrier, inc=1, device_id=friend, device_id_type=MESH)

    def colrange(xx):
        return pl.ds(pl.multiple_of(((25 * xx) // 2) * 128, 128), WIDE)

    def strip(zz, cc):
        return pl.ds(pl.multiple_of(zz * (NC * STRIP) + cc * STRIP, STRIP), STRIP)

    own_w = local(w_in.at[:, colrange(x)], wb.at[x, strip(z, c), :], xa_recv.at[0])
    own_w.start()
    own_h = local(h_in, hb.at[x, y], local_sem.at[0])
    own_h.start()
    own_t = local(t_in, tbuf.at[x], t_recv.at[0])
    own_t.start()
    own_c = local(c_in, cbuf, local_sem.at[1])
    own_c.start()
    pl.semaphore_wait(barrier, len(friends))

    for d in (1, 3, 2):
        xx = (x + d) % NX
        start(
            remote(
                w_in.at[:, colrange(xx)], wb.at[x, strip(z, c), :],
                xa_send.at[d], xa_recv.at[(NX - d) % NX], at(xx, y, z, c),
            )
        )

    def wait_cols(q):
        off = (q - x + NX) % NX
        local(w_in.at[:, colrange(0)], wb.at[q, strip(z, c), :], xa_recv.at[off]).wait()

    def span(path, part):
        first, count = SHARES[path, part]
        return pl.ds(first, count)

    def place(axis, along, cross, path, part):
        along, cross = (along + 4) % 4, (cross + 4) % 4
        xx, yy = (along, cross) if axis == 0 else (cross, along)
        return hb.at[xx, yy, span(path, part), :]

    def item(axis, d, j, me_along, cross):
        first, second = (0, 1) if axis == 0 else (1, 0)
        part = 0 if d == 1 else 1
        back = me_along - d
        if j == 0:
            return place(axis, me_along, cross, first, None)
        if j == 2:
            return place(axis, back, cross, first, part)
        if j in (1, 3, 5, 7):
            return place(axis, me_along, cross + {1: 0, 3: 1, 5: -1, 7: 2}[j], second, None)
        return place(axis, back, cross + {4: 0, 6: 1, 8: -1, 9: 2}[j], second, part)

    def links():
        for axis in (0, 1):
            for d in (1, -1):
                yield axis, d, 2 * axis + (0 if d == 1 else 1)

    def coords(axis):
        return (x, y) if axis == 0 else (y, x)

    def neighbour(axis, d):
        return at(x + d, y, z, c) if axis == 0 else at(x, y + d, z, c)

    def send_h(j):
        for axis, d, n in links():
            along, cross = coords(axis)
            dst = item(axis, d, j, along, cross)
            first, second = (0, 1) if axis == 0 else (1, 0)
            src = dst
            if j == 0:
                src = h_in.at[span(first, None), :]
            if j == 1:
                src = h_in.at[span(second, None), :]
            start(remote(src, dst, h_send.at[n, j], h_recv.at[n, j], neighbour(axis, d)))

    def wait_h(j):
        for axis, d, n in links():
            along, cross = coords(axis)
            got = item(axis, d, j, along - d, cross)
            remote(got, got, h_send.at[n, j], h_recv.at[n, j], neighbour(axis, d)).wait_recv()

    send_h(0)
    send_h(1)

    for d in (1, 2, 3):
        start(
            remote(t_in, tbuf.at[x], t_send.at[d], t_recv.at[(NX - d) % NX], at(x + d, y, z, c))
        )

    far = ((y - x + 4) % 4) // 2
    order = [(y + far) % 4, (y + 1 - far) % 4, (y + 3) % 4, (y + 2) % 4]

    def zitem(d, j):
        pair, i = divmod(j, 7)
        turn = 0 if d == 1 else 1
        return 2 * pair + (i + turn) % 2, i // 2

    def send_core(o, hops):
        ref = wb.at[order[o], strip((z - hops + NZ) % NZ, c), :]
        n = o * NZ + hops % NZ
        start(remote(ref, ref, c_send.at[n], c_recv.at[n], at(x, y, z, c + 1)))

    def wait_core(o):
        for hops in range(NZ):
            ref = wb.at[order[o], strip((z - hops + NZ) % NZ, (c + 1) % NC), :]
            n = o * NZ + hops
            remote(ref, ref, c_send.at[n], c_recv.at[n], at(x, y, z, c + 1)).wait_recv()

    def send_z(j, d):
        o, k = zitem(d, j)
        i = 0 if d == 1 else 1
        ref = wb.at[order[o], strip((z - d * k + NZ) % NZ, c), :]
        start(remote(ref, ref, z_send.at[i, j], z_recv.at[i, j], at(x, y, z + d, c)))

    def own_cols(o):
        wait_cols(order[o])
        send_core(o, 0)

    def step_z(j):
        for i, d in enumerate((1, -1)):
            o, k = zitem(d, j)
            ref = wb.at[order[o], strip((z - d * (k + 1) + NZ) % NZ, c), :]
            remote(ref, ref, z_send.at[i, j], z_recv.at[i, j], at(x, y, z + d, c)).wait_recv()
            if j + 2 == 7 and d == 1:
                own_cols(2)
                own_cols(3)
            if j + 2 < ZITEMS:
                send_z(j + 2, d)
        for d in (1, -1):
            o, k = zitem(d, j)
            send_core(o, d * (k + 1))

    own_cols(0)
    send_z(0, 1)
    send_z(1, -1)
    own_cols(1)
    send_z(0, -1)
    send_z(1, 1)

    odd = (x % 2).astype(jnp.float32)
    keep = 1.0 - odd
    away = odd * 1048576.0
    base = (y * COLS + ((25 * x) // 2) * 128).astype(jnp.float32)

    def prepare():
        own_c.wait()
        cpad[...] = jnp.zeros(cpad.shape, jnp.float32)
        for i in range(RES):
            cpad[pl.ds(i, 1), :] = cbuf[i].astype(jnp.float32)
        call[y] = cpad[...].astype(jnp.bfloat16)
        for d in (1, 3, 2):
            ref = call.at[y]
            start(remote(ref, ref, n_send.at[d], n_recv.at[(NY - d) % NY], at(x, y + d, z, c)))
        own_t.wait()
        for d in (1, 2, 3):
            ref = tbuf.at[(x + d) % NX]
            remote(ref, ref, t_send.at[d], t_recv.at[d], at(x + d, y, z, c)).wait_recv()
        lane = lax.broadcasted_iota(jnp.int32, (ROWS, 128), 1).astype(jnp.float32)
        for b in range(NX):
            t = tbuf[b].astype(jnp.float32) - base
            tsub[b] = jnp.broadcast_to(t, (128, ROWS)).T - lane

    def block(dx):
        return (x + dx) % NX

    def unit(dx, pair):
        b, ka, kb = block(dx), order[2 * pair], order[2 * pair + 1]
        part = jnp.dot(hb[b, ka], wb[ka], preferred_element_type=jnp.float32)
        part = part + jnp.dot(hb[b, kb], wb[kb], preferred_element_type=jnp.float32)
        if pair == 0:
            acc[b] = part
        else:
            acc[b] += part

    def finish(dx):
        b = block(dx)

        lane = lax.broadcasted_iota(jnp.int32, (64, 128), 1)
        halves = []
        for half in range(2):
            packed = jnp.zeros((64, 128), jnp.float32)
            for group in range(4):
                rows = pl.ds(group * 128 + half * 64, 64)

                def piece(j):
                    return acc[b, rows, pl.ds(j * 128, 128)]

                top = piece(0)
                for j in range(1, TILES):
                    top = jnp.maximum(top, piece(j))
                top = jnp.broadcast_to(jnp.max(top, axis=1, keepdims=True), (64, 128))
                want = tsub[b, rows, :]
                total = jnp.exp(piece(0) - top) * keep
                picked = jnp.where(want + away == 0.0, piece(0), 0.0)
                for j in range(1, TILES):
                    value = piece(j)
                    total = total + jnp.exp(value - top)
                    picked = jnp.where(want == j * 128.0, value, picked)
                total = jnp.sum(total, axis=1, keepdims=True)
                picked = jnp.sum(picked, axis=1, keepdims=True)
                for k, value in enumerate((top, total, picked)):
                    packed = jnp.where(lane == group + 4 * k, value, packed)
            halves.append(packed)
        sbuf[b] = jnp.concatenate(halves, axis=0).T[:16]
        for dy in (2, 1, 3, 0):
            n = dx * NY + dy
            m = ((NX - dx) % NX) * NY + (NY - dy) % NY
            if n:
                start(remote(sbuf.at[b], stats.at[m], s_send.at[n], s_recv.at[m], at(b, y + dy, z, c)))

    wait_h(0)
    send_h(2)
    send_h(3)
    step_z(0)
    step_z(1)
    step_z(2)
    wait_h(1)
    send_h(4)
    step_z(3)
    prepare()
    wait_h(2)
    send_h(5)
    step_z(4)
    step_z(5)
    step_z(6)
    wait_h(3)
    send_h(6)
    own_h.wait()
    wait_core(0)
    wait_core(1)
    step_z(7)
    wait_h(4)
    send_h(7)
    step_z(8)
    unit(0, 0)
    step_z(9)
    wait_h(5)
    send_h(8)
    step_z(10)
    unit(1, 0)
    wait_h(6)
    step_z(11)
    step_z(12)
    wait_h(7)
    send_h(9)
    step_z(13)
    unit(3, 0)
    wait_core(2)
    wait_core(3)
    unit(0, 1)
    unit(2, 0)
    wait_h(8)
    finish(0)
    unit(1, 1)
    finish(1)
    unit(3, 1)
    finish(3)
    wait_h(9)
    unit(2, 1)
    finish(2)

    drain()
    for d in (1, 2, 3):
        ref = call.at[(y + d) % NY]
        remote(ref, ref, n_send.at[d], n_recv.at[d], at(x, y + d, z, c)).wait_recv()
    for n in range(1, NX * NY):
        ref = stats.at[n]
        remote(ref, ref, s_send.at[n], s_recv.at[n], at(x, y, z, c)).wait_recv()

    parts = [sbuf[x]] + [stats[n] for n in range(1, NX * NY)]
    tops = [p[0:4] for p in parts]
    top = tops[0]
    for t in tops[1:]:
        top = jnp.maximum(top, t)
    total = jnp.zeros((4, 128), jnp.float32)
    target = jnp.zeros((4, 128), jnp.float32)
    for p, t in zip(parts, tops):
        total = total + p[4:8] * jnp.exp(t - top)
        target = target + p[8:12]
    ce = top + jnp.log(total) - target
    ce_out[...] = ce

    ce = jnp.concatenate([ce[g : g + 1] for g in range(4)], axis=1)
    high = ce.astype(jnp.bfloat16).astype(jnp.float32)
    middle = (ce - high).astype(jnp.bfloat16).astype(jnp.float32)
    low = (ce - high) - middle
    which = lax.broadcasted_iota(jnp.int32, (16, ROWS), 0)
    pieces = jnp.where(which == 0, high, jnp.where(which == 1, middle, jnp.where(which == 2, low, 0.0)))
    pieces = pieces.astype(jnp.bfloat16)

    def means_of(rhs):
        sums = lax.dot_general(
            pieces, rhs, (((1,), (1,)), ((), ())), preferred_element_type=jnp.float32
        )
        return jnp.sum(sums, axis=0, keepdims=True) * (1.0 / 32768.0)

    means = means_of(call[...].reshape(128, ROWS))
    lanes = lax.broadcasted_iota(jnp.int32, (1, 128), 1)
    mine1[...] = jnp.where(lanes % 32 < RES, means, BIG)

    others = [(dx, dc) for dx in range(NX) for dc in range(NC) if (dx, dc) != (0, 0)]
    for dx, dc in others:
        n, m = dx * NC + dc, ((NX - dx) % NX) * NC + dc
        start(remote(mine1, rows1.at[m], g_send.at[n], g_recv.at[m], at(x + dx, y, z, c + dc)))
    mean_out[...] = means_of(call[y])[:, :RES]
    mine2[pl.ds(0, 1), :] = mine1[...]
    for dx, dc in others:
        n = dx * NC + dc
        ref = rows1.at[n]
        remote(ref, ref, g_send.at[n], g_recv.at[n], at(x + dx, y, z, c + dc)).wait_recv()
        mine2[pl.ds(n, 1), :] = rows1[n]
    for d in (4, 3, 5, 2, 6, 1, 7):
        m = NZ - d
        start(remote(mine2, rows2.at[m], k_send.at[d], k_recv.at[m], at(x, y, z + d, c)))
    rows2[0] = mine2[...]
    for d in (1, 7, 2, 6, 3, 5, 4):
        ref = rows2.at[d]
        remote(ref, ref, k_send.at[d], k_recv.at[d], at(x, y, z + d, c)).wait_recv()

    col = lax.broadcasted_iota(jnp.int32, (8, 128), 1)
    rowi = lax.broadcasted_iota(jnp.int32, (8, 128), 0)
    want = jnp.zeros((8, 128), jnp.float32)
    for q in range(8):
        want = jnp.where(rowi == q, ranks[q].astype(jnp.float32), want)

    def below(cands):
        counts = [jnp.zeros((8, 128), jnp.float32) for _ in cands]
        for n in range(NZ):
            for r in range(8):
                v = jnp.broadcast_to(rows2[n, pl.ds(r, 1), :], (8, 128))
                counts = [k + jnp.where(v < t, 1.0, 0.0) for k, t in zip(counts, cands)]
        return [jnp.broadcast_to(jnp.sum(k, axis=1, keepdims=True), (8, 128)) for k in counts]

    def pick(lo, cands):
        for k, t in zip(below(cands), cands):
            lo = jnp.where(k <= want, t, lo)
        return lo

    tiny = 2.0**-126
    lo = jnp.full((8, 128), tiny, jnp.float32)
    for e in (64, 16, 4, 1):
        first = lo * 2.0**e
        lo = pick(lo, [first, first * 2.0**e, first * 2.0**e * 2.0**e])
    unit0 = lo

    def refine(_, carry):
        lo, part = carry
        quarter = part * 0.25
        return pick(lo, [lo + quarter, lo + 2.0 * quarter, lo + 3.0 * quarter]), quarter

    lo, part = lax.fori_loop(0, 11, refine, (lo, unit0))
    lo = pick(lo, [lo + part * 0.5])
    none = below([jnp.full((8, 128), tiny, jnp.float32)])[0] > want
    lo = jnp.where(none, 0.0, lo)
    q_out[...] = jnp.sum(jnp.where(col == rowi, lo, 0.0), axis=0, keepdims=True)[:, :8]
    drain()


def shards(hidden, proj_weight, targets, counts, ranks):
    f32, bf16, i32 = jnp.float32, jnp.bfloat16, jnp.int32
    dma = pltpu.SemaphoreType.DMA
    hbm = pl.BlockSpec(memory_space=pl.ANY)
    vmem = pl.BlockSpec(memory_space=pltpu.VMEM)
    ce, means, quantiles = pl.pallas_call(
        kernel,
        out_shape=(
            jax.ShapeDtypeStruct((4, 128), f32),
            jax.ShapeDtypeStruct((1, RES), f32),
            jax.ShapeDtypeStruct((1, 8), f32),
        ),
        in_specs=[pl.BlockSpec(memory_space=pltpu.SMEM), hbm, hbm, hbm, hbm],
        out_specs=(vmem, vmem, vmem),
        scratch_shapes=[
            pltpu.VMEM((NX, NY, ROWS, KB), bf16),
            pltpu.VMEM((4, KB, WIDE), bf16),
            pltpu.VMEM((NX, ROWS, WIDE), f32),
            pltpu.VMEM((NX, ROWS, 128), f32),
            pltpu.VMEM((NX, 1, ROWS), i32),
            pltpu.VMEM((RES, 1, ROWS), i32),
            pltpu.VMEM((32, ROWS), f32),
            pltpu.VMEM((NY, 32, ROWS), bf16),
            pltpu.VMEM((NX, 16, 128), f32),
            pltpu.VMEM((NX * NY, 16, 128), f32),
            pltpu.VMEM((8, 1, 128), f32),
            pltpu.VMEM((1, 128), f32),
            pltpu.VMEM((NZ, 8, 128), f32),
            pltpu.VMEM((8, 128), f32),
            dma((2,)),
            dma((4,)), dma((4,)),
            dma((4,)), dma((4,)),
            dma((4, ITEMS)), dma((4, ITEMS)),
            dma((2, ZITEMS)), dma((2, ZITEMS)),
            dma((4 * NZ,)), dma((4 * NZ,)),
            dma((4,)), dma((4,)),
            dma((16,)), dma((16,)),
            dma((8,)), dma((8,)),
            dma((8,)), dma((8,)),
        ],
        compiler_params=pltpu.CompilerParams(
            collective_id=0, has_side_effects=True, vmem_limit_bytes=60 * 2**20
        ),
    )(ranks, hidden, proj_weight, targets.reshape(1, ROWS), counts.transpose(1, 0, 2))
    return ce.reshape(ROWS), means, quantiles.reshape(8)


def solution(mesh):
    return jax.shard_map(
        shards,
        mesh=mesh,
        in_specs=(
            P("subset", "vocab"),
            P("subset", "vocab"),
            P("subset"),
            P("subset", "vocab", None),
            P(),
        ),
        out_specs=(P("subset"), P("subset", "vocab"), P()),
        check_vma=False,
    )
```

```python
import jax
import jax.numpy as jnp
from jax import lax
from jax.experimental import pallas as pl
from jax.experimental.pallas import tpu as pltpu
from jax.sharding import PartitionSpec as P

MESH = pl.DeviceIdType.MESH
NX, NY, NZ, NC = 4, 4, 8, 2
ROWS = 512
SHARES = {
    (0, None): (0, 272), (0, 0): (0, 144), (0, 1): (144, 128),
    (1, None): (272, 240), (1, 0): (272, 128), (1, 1): (400, 112),
}
KB = 512
COLS = 6400
TILES = 13
WIDE = TILES * 128
STRIP = 32
RES = 25
ITEMS = 10
ZITEMS = 14
BIG = 3.0e38


def kernel(
    ranks, h_in, w_in, t_in, c_in,
    ce_out, mean_out, q_out,
    hb, wb, acc, tsub, tbuf, cbuf, cpad, call, sbuf, stats, rows1, mine1, rows2, mine2,
    local_sem, xa_send, xa_recv, t_send, t_recv, h_send, h_recv, z_send, z_recv, c_send, c_recv,
    n_send, n_recv, s_send, s_recv, g_send, g_recv, k_send, k_recv,
):
    sub = lax.axis_index("subset")
    y = lax.axis_index("vocab")
    x = sub // (NZ * NC)
    z = (sub // NC) % NZ
    c = sub % NC

    def at(xx, yy, zz, cc):
        return (((xx + NX) % NX) * (NZ * NC) + ((zz + NZ) % NZ) * NC + (cc + NC) % NC, (yy + NY) % NY)

    def remote(src, dst, ss, rs, dev):
        return pltpu.make_async_remote_copy(
            src_ref=src, dst_ref=dst, send_sem=ss, recv_sem=rs, device_id=dev, device_id_type=MESH
        )

    def local(src, dst, sem):
        return pltpu.make_async_copy(src, dst, sem)

    sends = []

    def start(copy):
        copy.start()
        sends.append(copy)

    def drain():
        for copy in sends:
            copy.wait_send()
        sends.clear()

    barrier = pltpu.get_barrier_semaphore()
    friends = [
        at(x + 1, y, z, c), at(x + 2, y, z, c), at(x + 3, y, z, c), at(x, y + 1, z, c), at(x, y + 3, z, c),
        at(x, y, z + 1, c), at(x, y, z - 1, c), at(x, y, z, c + 1),
    ]
    for friend in friends:
        pl.semaphore_signal(barrier, inc=1, device_id=friend, device_id_type=MESH)

    def colrange(xx):
        return pl.ds(pl.multiple_of(((25 * xx) // 2) * 128, 128), WIDE)

    def strip(zz, cc):
        return pl.ds(pl.multiple_of(zz * (NC * STRIP) + cc * STRIP, STRIP), STRIP)

    own_w = local(w_in.at[:, colrange(x)], wb.at[x, strip(z, c), :], xa_recv.at[0])
    own_w.start()
    own_h = local(h_in, hb.at[x, y], local_sem.at[0])
    own_h.start()
    own_t = local(t_in, tbuf.at[x], t_recv.at[0])
    own_t.start()
    own_c = local(c_in, cbuf, local_sem.at[1])
    own_c.start()
    pl.semaphore_wait(barrier, len(friends))

    for d in (1, 3, 2):
        xx = (x + d) % NX
        start(
            remote(
                w_in.at[:, colrange(xx)], wb.at[x, strip(z, c), :],
                xa_send.at[d], xa_recv.at[(NX - d) % NX], at(xx, y, z, c),
            )
        )

    def wait_cols(q):
        off = (q - x + NX) % NX
        local(w_in.at[:, colrange(0)], wb.at[q, strip(z, c), :], xa_recv.at[off]).wait()

    def span(path, part):
        first, count = SHARES[path, part]
        return pl.ds(first, count)

    def place(axis, along, cross, path, part):
        along, cross = (along + 4) % 4, (cross + 4) % 4
        xx, yy = (along, cross) if axis == 0 else (cross, along)
        return hb.at[xx, yy, span(path, part), :]

    def item(axis, d, j, me_along, cross):
        first, second = (0, 1) if axis == 0 else (1, 0)
        part = 0 if d == 1 else 1
        back = me_along - d
        if j == 0:
            return place(axis, me_along, cross, first, None)
        if j == 2:
            return place(axis, back, cross, first, part)
        if j in (1, 3, 5, 7):
            return place(axis, me_along, cross + {1: 0, 3: 1, 5: -1, 7: 2}[j], second, None)
        return place(axis, back, cross + {4: 0, 6: 1, 8: -1, 9: 2}[j], second, part)

    def links():
        for axis in (0, 1):
            for d in (1, -1):
                yield axis, d, 2 * axis + (0 if d == 1 else 1)

    def coords(axis):
        return (x, y) if axis == 0 else (y, x)

    def neighbour(axis, d):
        return at(x + d, y, z, c) if axis == 0 else at(x, y + d, z, c)

    def send_h(j):
        for axis, d, n in links():
            along, cross = coords(axis)
            dst = item(axis, d, j, along, cross)
            first, second = (0, 1) if axis == 0 else (1, 0)
            src = dst
            if j == 0:
                src = h_in.at[span(first, None), :]
            if j == 1:
                src = h_in.at[span(second, None), :]
            start(remote(src, dst, h_send.at[n, j], h_recv.at[n, j], neighbour(axis, d)))

    def wait_h(j):
        for axis, d, n in links():
            along, cross = coords(axis)
            got = item(axis, d, j, along - d, cross)
            remote(got, got, h_send.at[n, j], h_recv.at[n, j], neighbour(axis, d)).wait_recv()

    send_h(0)
    send_h(1)

    for d in (1, 2, 3):
        start(
            remote(t_in, tbuf.at[x], t_send.at[d], t_recv.at[(NX - d) % NX], at(x + d, y, z, c))
        )

    far = ((y - x + 4) % 4) // 2
    order = [(y + far) % 4, (y + 1 - far) % 4, (y + 3) % 4, (y + 2) % 4]

    def zitem(d, j):
        pair, i = divmod(j, 7)
        turn = 0 if d == 1 else 1
        return 2 * pair + (i + turn) % 2, i // 2

    def send_core(o, hops):
        ref = wb.at[order[o], strip((z - hops + NZ) % NZ, c), :]
        n = o * NZ + hops % NZ
        start(remote(ref, ref, c_send.at[n], c_recv.at[n], at(x, y, z, c + 1)))

    def wait_core(o):
        for hops in range(NZ):
            ref = wb.at[order[o], strip((z - hops + NZ) % NZ, (c + 1) % NC), :]
            n = o * NZ + hops
            remote(ref, ref, c_send.at[n], c_recv.at[n], at(x, y, z, c + 1)).wait_recv()

    def send_z(j, d):
        o, k = zitem(d, j)
        i = 0 if d == 1 else 1
        ref = wb.at[order[o], strip((z - d * k + NZ) % NZ, c), :]
        start(remote(ref, ref, z_send.at[i, j], z_recv.at[i, j], at(x, y, z + d, c)))

    def own_cols(o):
        wait_cols(order[o])
        send_core(o, 0)

    def step_z(j):
        for i, d in enumerate((1, -1)):
            o, k = zitem(d, j)
            ref = wb.at[order[o], strip((z - d * (k + 1) + NZ) % NZ, c), :]
            remote(ref, ref, z_send.at[i, j], z_recv.at[i, j], at(x, y, z + d, c)).wait_recv()
            if j + 2 == 7 and d == 1:
                own_cols(2)
                own_cols(3)
            if j + 2 < ZITEMS:
                send_z(j + 2, d)
        for d in (1, -1):
            o, k = zitem(d, j)
            send_core(o, d * (k + 1))

    own_cols(0)
    send_z(0, 1)
    send_z(1, -1)
    own_cols(1)
    send_z(0, -1)
    send_z(1, 1)

    odd = (x % 2).astype(jnp.float32)
    keep = 1.0 - odd
    away = odd * 1048576.0
    base = (y * COLS + ((25 * x) // 2) * 128).astype(jnp.float32)

    def prepare():
        own_c.wait()
        cpad[...] = jnp.zeros(cpad.shape, jnp.float32)
        for i in range(RES):
            cpad[pl.ds(i, 1), :] = cbuf[i].astype(jnp.float32)
        call[y] = cpad[...].astype(jnp.bfloat16)
        for d in (1, 3, 2):
            ref = call.at[y]
            start(remote(ref, ref, n_send.at[d], n_recv.at[(NY - d) % NY], at(x, y + d, z, c)))
        own_t.wait()
        for d in (1, 2, 3):
            ref = tbuf.at[(x + d) % NX]
            remote(ref, ref, t_send.at[d], t_recv.at[d], at(x + d, y, z, c)).wait_recv()
        lane = lax.broadcasted_iota(jnp.int32, (ROWS, 128), 1).astype(jnp.float32)
        for b in range(NX):
            t = tbuf[b].astype(jnp.float32) - base
            tsub[b] = jnp.broadcast_to(t, (128, ROWS)).T - lane

    def block(dx):
        return (x + dx) % NX

    def unit(dx, pair):
        b, ka, kb = block(dx), order[2 * pair], order[2 * pair + 1]
        part = jnp.dot(hb[b, ka], wb[ka], preferred_element_type=jnp.float32)
        part = part + jnp.dot(hb[b, kb], wb[kb], preferred_element_type=jnp.float32)
        if pair == 0:
            acc[b] = part
        else:
            acc[b] += part

    def finish(dx):
        b = block(dx)

        lane = lax.broadcasted_iota(jnp.int32, (64, 128), 1)
        halves = []
        for half in range(2):
            packed = jnp.zeros((64, 128), jnp.float32)
            for group in range(4):
                rows = pl.ds(group * 128 + half * 64, 64)

                def piece(j):
                    return acc[b, rows, pl.ds(j * 128, 128)]

                top = piece(0)
                for j in range(1, TILES):
                    top = jnp.maximum(top, piece(j))
                top = jnp.broadcast_to(jnp.max(top, axis=1, keepdims=True), (64, 128))
                want = tsub[b, rows, :]
                total = jnp.exp(piece(0) - top) * keep
                picked = jnp.where(want + away == 0.0, piece(0), 0.0)
                for j in range(1, TILES):
                    value = piece(j)
                    total = total + jnp.exp(value - top)
                    picked = jnp.where(want == j * 128.0, value, picked)
                total = jnp.sum(total, axis=1, keepdims=True)
                picked = jnp.sum(picked, axis=1, keepdims=True)
                for k, value in enumerate((top, total, picked)):
                    packed = jnp.where(lane == group + 4 * k, value, packed)
            halves.append(packed)
        sbuf[b] = jnp.concatenate(halves, axis=0).T[:16]
        for dy in (2, 1, 3, 0):
            n = dx * NY + dy
            m = ((NX - dx) % NX) * NY + (NY - dy) % NY
            if n:
                start(remote(sbuf.at[b], stats.at[m], s_send.at[n], s_recv.at[m], at(b, y + dy, z, c)))

    wait_h(0)
    send_h(2)
    send_h(3)
    step_z(0)
    step_z(1)
    step_z(2)
    wait_h(1)
    send_h(4)
    step_z(3)
    prepare()
    wait_h(2)
    send_h(5)
    step_z(4)
    step_z(5)
    step_z(6)
    wait_h(3)
    send_h(6)
    own_h.wait()
    wait_core(0)
    wait_core(1)
    step_z(7)
    wait_h(4)
    send_h(7)
    step_z(8)
    unit(0, 0)
    step_z(9)
    wait_h(5)
    send_h(8)
    step_z(10)
    unit(1, 0)
    wait_h(6)
    step_z(11)
    unit(3, 0)
    step_z(12)
    wait_h(7)
    send_h(9)
    step_z(13)
    wait_core(2)
    wait_core(3)
    unit(0, 1)
    unit(2, 0)
    wait_h(8)
    finish(0)
    unit(1, 1)
    finish(1)
    unit(3, 1)
    finish(3)
    wait_h(9)
    unit(2, 1)
    finish(2)

    drain()
    for d in (1, 2, 3):
        ref = call.at[(y + d) % NY]
        remote(ref, ref, n_send.at[d], n_recv.at[d], at(x, y + d, z, c)).wait_recv()
    for n in range(1, NX * NY):
        ref = stats.at[n]
        remote(ref, ref, s_send.at[n], s_recv.at[n], at(x, y, z, c)).wait_recv()

    parts = [sbuf[x]] + [stats[n] for n in range(1, NX * NY)]
    tops = [p[0:4] for p in parts]
    top = tops[0]
    for t in tops[1:]:
        top = jnp.maximum(top, t)
    total = jnp.zeros((4, 128), jnp.float32)
    target = jnp.zeros((4, 128), jnp.float32)
    for p, t in zip(parts, tops):
        total = total + p[4:8] * jnp.exp(t - top)
        target = target + p[8:12]
    ce = top + jnp.log(total) - target
    ce_out[...] = ce

    ce = jnp.concatenate([ce[g : g + 1] for g in range(4)], axis=1)
    high = ce.astype(jnp.bfloat16).astype(jnp.float32)
    middle = (ce - high).astype(jnp.bfloat16).astype(jnp.float32)
    low = (ce - high) - middle
    which = lax.broadcasted_iota(jnp.int32, (16, ROWS), 0)
    pieces = jnp.where(which == 0, high, jnp.where(which == 1, middle, jnp.where(which == 2, low, 0.0)))
    pieces = pieces.astype(jnp.bfloat16)

    def means_of(rhs):
        sums = lax.dot_general(
            pieces, rhs, (((1,), (1,)), ((), ())), preferred_element_type=jnp.float32
        )
        return jnp.sum(sums, axis=0, keepdims=True) * (1.0 / 32768.0)

    means = means_of(call[...].reshape(128, ROWS))
    lanes = lax.broadcasted_iota(jnp.int32, (1, 128), 1)
    mine1[...] = jnp.where(lanes % 32 < RES, means, BIG)

    others = [(dx, dc) for dx in range(NX) for dc in range(NC) if (dx, dc) != (0, 0)]
    for dx, dc in others:
        n, m = dx * NC + dc, ((NX - dx) % NX) * NC + dc
        start(remote(mine1, rows1.at[m], g_send.at[n], g_recv.at[m], at(x + dx, y, z, c + dc)))
    mean_out[...] = means_of(call[y])[:, :RES]
    mine2[pl.ds(0, 1), :] = mine1[...]
    for dx, dc in others:
        n = dx * NC + dc
        ref = rows1.at[n]
        remote(ref, ref, g_send.at[n], g_recv.at[n], at(x + dx, y, z, c + dc)).wait_recv()
        mine2[pl.ds(n, 1), :] = rows1[n]
    for d in (4, 3, 5, 2, 6, 1, 7):
        m = NZ - d
        start(remote(mine2, rows2.at[m], k_send.at[d], k_recv.at[m], at(x, y, z + d, c)))
    rows2[0] = mine2[...]
    for d in (1, 7, 2, 6, 3, 5, 4):
        ref = rows2.at[d]
        remote(ref, ref, k_send.at[d], k_recv.at[d], at(x, y, z + d, c)).wait_recv()

    col = lax.broadcasted_iota(jnp.int32, (8, 128), 1)
    rowi = lax.broadcasted_iota(jnp.int32, (8, 128), 0)
    want = jnp.zeros((8, 128), jnp.float32)
    for q in range(8):
        want = jnp.where(rowi == q, ranks[q].astype(jnp.float32), want)

    def below(cands):
        counts = [jnp.zeros((8, 128), jnp.float32) for _ in cands]
        for n in range(NZ):
            for r in range(8):
                v = jnp.broadcast_to(rows2[n, pl.ds(r, 1), :], (8, 128))
                counts = [k + jnp.where(v < t, 1.0, 0.0) for k, t in zip(counts, cands)]
        return [jnp.broadcast_to(jnp.sum(k, axis=1, keepdims=True), (8, 128)) for k in counts]

    def pick(lo, cands):
        for k, t in zip(below(cands), cands):
            lo = jnp.where(k <= want, t, lo)
        return lo

    tiny = 2.0**-126
    lo = jnp.full((8, 128), tiny, jnp.float32)
    for e in (64, 16, 4, 1):
        first = lo * 2.0**e
        lo = pick(lo, [first, first * 2.0**e, first * 2.0**e * 2.0**e])
    unit0 = lo

    def refine(_, carry):
        lo, part = carry
        quarter = part * 0.25
        return pick(lo, [lo + quarter, lo + 2.0 * quarter, lo + 3.0 * quarter]), quarter

    lo, part = lax.fori_loop(0, 11, refine, (lo, unit0))
    lo = pick(lo, [lo + part * 0.5])
    none = below([jnp.full((8, 128), tiny, jnp.float32)])[0] > want
    lo = jnp.where(none, 0.0, lo)
    q_out[...] = jnp.sum(jnp.where(col == rowi, lo, 0.0), axis=0, keepdims=True)[:, :8]
    drain()


def emit(ce_in, mean_in, q_in, ce_out, mean_out, q_out, sem):
    copies = [
        pltpu.make_async_copy(src, dst, sem.at[i])
        for i, (src, dst) in enumerate(((ce_in, ce_out), (mean_in, mean_out), (q_in, q_out)))
    ]
    for copy in copies:
        copy.start()
    for copy in copies:
        copy.wait()


def shards(hidden, proj_weight, targets, counts, ranks):
    f32, bf16, i32 = jnp.float32, jnp.bfloat16, jnp.int32
    dma = pltpu.SemaphoreType.DMA
    hbm = pl.BlockSpec(memory_space=pl.ANY)
    vmem = pl.BlockSpec(memory_space=pltpu.VMEM)
    ce, means, quantiles = pl.pallas_call(
        kernel,
        out_shape=(
            jax.ShapeDtypeStruct((4, 128), f32),
            jax.ShapeDtypeStruct((1, RES), f32),
            jax.ShapeDtypeStruct((1, 8), f32),
        ),
        in_specs=[pl.BlockSpec(memory_space=pltpu.SMEM), hbm, hbm, hbm, hbm],
        out_specs=(vmem, vmem, vmem),
        scratch_shapes=[
            pltpu.VMEM((NX, NY, ROWS, KB), bf16),
            pltpu.VMEM((4, KB, WIDE), bf16),
            pltpu.VMEM((NX, ROWS, WIDE), f32),
            pltpu.VMEM((NX, ROWS, 128), f32),
            pltpu.VMEM((NX, 1, ROWS), i32),
            pltpu.VMEM((RES, 1, ROWS), i32),
            pltpu.VMEM((32, ROWS), f32),
            pltpu.VMEM((NY, 32, ROWS), bf16),
            pltpu.VMEM((NX, 16, 128), f32),
            pltpu.VMEM((NX * NY, 16, 128), f32),
            pltpu.VMEM((8, 1, 128), f32),
            pltpu.VMEM((1, 128), f32),
            pltpu.VMEM((NZ, 8, 128), f32),
            pltpu.VMEM((8, 128), f32),
            dma((2,)),
            dma((4,)), dma((4,)),
            dma((4,)), dma((4,)),
            dma((4, ITEMS)), dma((4, ITEMS)),
            dma((2, ZITEMS)), dma((2, ZITEMS)),
            dma((4 * NZ,)), dma((4 * NZ,)),
            dma((4,)), dma((4,)),
            dma((16,)), dma((16,)),
            dma((8,)), dma((8,)),
            dma((8,)), dma((8,)),
        ],
        compiler_params=pltpu.CompilerParams(
            collective_id=0, has_side_effects=True, vmem_limit_bytes=60 * 2**20
        ),
    )(ranks, hidden, proj_weight, targets.reshape(1, ROWS), counts.transpose(1, 0, 2))
    ce, means, quantiles = pl.pallas_call(
        emit,
        out_shape=(
            jax.ShapeDtypeStruct((ROWS,), f32),
            jax.ShapeDtypeStruct((1, RES), f32),
            jax.ShapeDtypeStruct((8,), f32),
        ),
        in_specs=[hbm, hbm, hbm],
        out_specs=(hbm, hbm, hbm),
        scratch_shapes=[dma((3,))],
    )(ce.reshape(ROWS), means, quantiles.reshape(8))
    return ce, means, quantiles


def solution(mesh):
    return jax.shard_map(
        shards,
        mesh=mesh,
        in_specs=(
            P("subset", "vocab"),
            P("subset", "vocab"),
            P("subset"),
            P("subset", "vocab", None),
            P(),
        ),
        out_specs=(P("subset"), P("subset", "vocab"), P()),
        check_vma=False,
    )
```

```python
import jax
import jax.numpy as jnp
from jax import lax
from jax.experimental import pallas as pl
from jax.experimental.pallas import tpu as pltpu
from jax.sharding import PartitionSpec as P

MESH = pl.DeviceIdType.MESH
NX, NY, NZ, NC = 4, 4, 8, 2
ROWS = 512
SHARES = {
    (0, None): (0, 272), (0, 0): (0, 144), (0, 1): (144, 128),
    (1, None): (272, 240), (1, 0): (272, 128), (1, 1): (400, 112),
}
KB = 512
COLS = 6400
TILES = 13
WIDE = TILES * 128
STRIP = 32
RES = 25
ITEMS = 10
ZITEMS = 14
BIG = 3.0e38


def kernel(
    ranks, h_in, w_in, t_in, c_in,
    ce_out, mean_out, q_out,
    hb, wb, acc, tsub, tbuf, cbuf, cpad, call, sbuf, stats, rows1, mine1, rows2, mine2,
    local_sem, xa_send, xa_recv, t_send, t_recv, h_send, h_recv, z_send, z_recv, c_send, c_recv,
    n_send, n_recv, s_send, s_recv, g_send, g_recv, k_send, k_recv,
):
    sub = lax.axis_index("subset")
    y = lax.axis_index("vocab")
    x = sub // (NZ * NC)
    z = (sub // NC) % NZ
    c = sub % NC

    def at(xx, yy, zz, cc):
        return (((xx + NX) % NX) * (NZ * NC) + ((zz + NZ) % NZ) * NC + (cc + NC) % NC, (yy + NY) % NY)

    def remote(src, dst, ss, rs, dev):
        return pltpu.make_async_remote_copy(
            src_ref=src, dst_ref=dst, send_sem=ss, recv_sem=rs, device_id=dev, device_id_type=MESH
        )

    def local(src, dst, sem):
        return pltpu.make_async_copy(src, dst, sem)

    sends = []

    def start(copy):
        copy.start()
        sends.append(copy)

    def drain():
        for copy in sends:
            copy.wait_send()
        sends.clear()

    barrier = pltpu.get_barrier_semaphore()
    friends = [
        at(x + 1, y, z, c), at(x + 2, y, z, c), at(x + 3, y, z, c), at(x, y + 1, z, c), at(x, y + 3, z, c),
        at(x, y, z + 1, c), at(x, y, z - 1, c), at(x, y, z, c + 1),
    ]
    for friend in friends:
        pl.semaphore_signal(barrier, inc=1, device_id=friend, device_id_type=MESH)

    def colrange(xx):
        return pl.ds(pl.multiple_of(((25 * xx) // 2) * 128, 128), WIDE)

    def strip(zz, cc):
        return pl.ds(pl.multiple_of(zz * (NC * STRIP) + cc * STRIP, STRIP), STRIP)

    own_w = local(w_in.at[:, colrange(x)], wb.at[x, strip(z, c), :], xa_recv.at[0])
    own_w.start()
    own_h = local(h_in, hb.at[x, y], local_sem.at[0])
    own_h.start()
    own_t = local(t_in, tbuf.at[x], t_recv.at[0])
    own_t.start()
    own_c = local(c_in, cbuf, local_sem.at[1])
    own_c.start()
    pl.semaphore_wait(barrier, len(friends))

    for d in (1, 3, 2):
        xx = (x + d) % NX
        start(
            remote(
                w_in.at[:, colrange(xx)], wb.at[x, strip(z, c), :],
                xa_send.at[d], xa_recv.at[(NX - d) % NX], at(xx, y, z, c),
            )
        )

    def wait_cols(q):
        off = (q - x + NX) % NX
        local(w_in.at[:, colrange(0)], wb.at[q, strip(z, c), :], xa_recv.at[off]).wait()

    def span(path, part):
        first, count = SHARES[path, part]
        return pl.ds(first, count)

    def place(axis, along, cross, path, part):
        along, cross = (along + 4) % 4, (cross + 4) % 4
        xx, yy = (along, cross) if axis == 0 else (cross, along)
        return hb.at[xx, yy, span(path, part), :]

    def item(axis, d, j, me_along, cross):
        first, second = (0, 1) if axis == 0 else (1, 0)
        part = 0 if d == 1 else 1
        back = me_along - d
        if j == 0:
            return place(axis, me_along, cross, first, None)
        if j == 2:
            return place(axis, back, cross, first, part)
        if j in (1, 3, 5, 7):
            return place(axis, me_along, cross + {1: 0, 3: 1, 5: -1, 7: 2}[j], second, None)
        return place(axis, back, cross + {4: 0, 6: 1, 8: -1, 9: 2}[j], second, part)

    def links():
        for axis in (0, 1):
            for d in (1, -1):
                yield axis, d, 2 * axis + (0 if d == 1 else 1)

    def coords(axis):
        return (x, y) if axis == 0 else (y, x)

    def neighbour(axis, d):
        return at(x + d, y, z, c) if axis == 0 else at(x, y + d, z, c)

    def send_h(j):
        for axis, d, n in links():
            along, cross = coords(axis)
            dst = item(axis, d, j, along, cross)
            first, second = (0, 1) if axis == 0 else (1, 0)
            src = dst
            if j == 0:
                src = h_in.at[span(first, None), :]
            if j == 1:
                src = h_in.at[span(second, None), :]
            start(remote(src, dst, h_send.at[n, j], h_recv.at[n, j], neighbour(axis, d)))

    def wait_h(j):
        for axis, d, n in links():
            along, cross = coords(axis)
            got = item(axis, d, j, along - d, cross)
            remote(got, got, h_send.at[n, j], h_recv.at[n, j], neighbour(axis, d)).wait_recv()

    send_h(0)
    send_h(1)

    for d in (1, 2, 3):
        start(
            remote(t_in, tbuf.at[x], t_send.at[d], t_recv.at[(NX - d) % NX], at(x + d, y, z, c))
        )

    far = ((y - x + 4) % 4) // 2
    order = [(y + far) % 4, (y + 1 - far) % 4, (y + 3) % 4, (y + 2) % 4]

    def zitem(d, j):
        pair, i = divmod(j, 7)
        turn = 0 if d == 1 else 1
        return 2 * pair + (i + turn) % 2, i // 2

    def send_core(o, hops):
        ref = wb.at[order[o], strip((z - hops + NZ) % NZ, c), :]
        n = o * NZ + hops % NZ
        start(remote(ref, ref, c_send.at[n], c_recv.at[n], at(x, y, z, c + 1)))

    def wait_core(o):
        for hops in range(NZ):
            ref = wb.at[order[o], strip((z - hops + NZ) % NZ, (c + 1) % NC), :]
            n = o * NZ + hops
            remote(ref, ref, c_send.at[n], c_recv.at[n], at(x, y, z, c + 1)).wait_recv()

    def send_z(j, d):
        o, k = zitem(d, j)
        i = 0 if d == 1 else 1
        ref = wb.at[order[o], strip((z - d * k + NZ) % NZ, c), :]
        start(remote(ref, ref, z_send.at[i, j], z_recv.at[i, j], at(x, y, z + d, c)))

    def own_cols(o):
        wait_cols(order[o])
        send_core(o, 0)

    def step_z(j):
        for i, d in enumerate((1, -1)):
            o, k = zitem(d, j)
            ref = wb.at[order[o], strip((z - d * (k + 1) + NZ) % NZ, c), :]
            remote(ref, ref, z_send.at[i, j], z_recv.at[i, j], at(x, y, z + d, c)).wait_recv()
            if j + 2 == 7 and d == 1:
                own_cols(2)
                own_cols(3)
            if j + 2 < ZITEMS:
                send_z(j + 2, d)
        for d in (1, -1):
            o, k = zitem(d, j)
            send_core(o, d * (k + 1))

    own_cols(0)
    send_z(0, 1)
    send_z(1, -1)
    own_cols(1)
    send_z(0, -1)
    send_z(1, 1)

    odd = (x % 2).astype(jnp.float32)
    keep = 1.0 - odd
    away = odd * 1048576.0
    base = (y * COLS + ((25 * x) // 2) * 128).astype(jnp.float32)

    def prepare():
        own_c.wait()
        cpad[...] = jnp.zeros(cpad.shape, jnp.float32)
        for i in range(RES):
            cpad[pl.ds(i, 1), :] = cbuf[i].astype(jnp.float32)
        call[y] = cpad[...].astype(jnp.bfloat16)
        for d in (1, 3, 2):
            ref = call.at[y]
            start(remote(ref, ref, n_send.at[d], n_recv.at[(NY - d) % NY], at(x, y + d, z, c)))
        own_t.wait()
        for d in (1, 2, 3):
            ref = tbuf.at[(x + d) % NX]
            remote(ref, ref, t_send.at[d], t_recv.at[d], at(x + d, y, z, c)).wait_recv()
        lane = lax.broadcasted_iota(jnp.int32, (ROWS, 128), 1).astype(jnp.float32)
        for b in range(NX):
            t = tbuf[b].astype(jnp.float32) - base
            tsub[b] = jnp.broadcast_to(t, (128, ROWS)).T - lane

    def block(dx):
        return (x + dx) % NX

    def unit(dx, pair):
        b, ka, kb = block(dx), order[2 * pair], order[2 * pair + 1]
        part = jnp.dot(hb[b, ka], wb[ka], preferred_element_type=jnp.float32)
        part = part + jnp.dot(hb[b, kb], wb[kb], preferred_element_type=jnp.float32)
        if pair == 0:
            acc[b] = part
        else:
            acc[b] += part

    def finish(dx):
        b = block(dx)

        lane = lax.broadcasted_iota(jnp.int32, (64, 128), 1)
        halves = []
        for half in range(2):
            packed = jnp.zeros((64, 128), jnp.float32)
            for group in range(4):
                rows = pl.ds(group * 128 + half * 64, 64)

                def piece(j):
                    return acc[b, rows, pl.ds(j * 128, 128)]

                top = piece(0)
                for j in range(1, TILES):
                    top = jnp.maximum(top, piece(j))
                top = jnp.broadcast_to(jnp.max(top, axis=1, keepdims=True), (64, 128))
                want = tsub[b, rows, :]
                total = jnp.exp(piece(0) - top) * keep
                picked = jnp.where(want + away == 0.0, piece(0), 0.0)
                for j in range(1, TILES):
                    value = piece(j)
                    total = total + jnp.exp(value - top)
                    picked = jnp.where(want == j * 128.0, value, picked)
                total = jnp.sum(total, axis=1, keepdims=True)
                picked = jnp.sum(picked, axis=1, keepdims=True)
                for k, value in enumerate((top, total, picked)):
                    packed = jnp.where(lane == group + 4 * k, value, packed)
            halves.append(packed)
        sbuf[b] = jnp.concatenate(halves, axis=0).T[:16]
        for dy in (2, 1, 3, 0):
            n = dx * NY + dy
            m = ((NX - dx) % NX) * NY + (NY - dy) % NY
            if n:
                start(remote(sbuf.at[b], stats.at[m], s_send.at[n], s_recv.at[m], at(b, y + dy, z, c)))

    wait_h(0)
    send_h(2)
    step_z(0)
    step_z(1)
    step_z(2)
    wait_h(1)
    send_h(3)
    send_h(4)
    step_z(3)
    prepare()
    wait_h(2)
    send_h(5)
    step_z(4)
    step_z(5)
    step_z(6)
    wait_h(3)
    send_h(6)
    own_h.wait()
    wait_core(0)
    wait_core(1)
    step_z(7)
    wait_h(4)
    send_h(7)
    step_z(8)
    unit(0, 0)
    step_z(9)
    wait_h(5)
    send_h(8)
    step_z(10)
    unit(1, 0)
    wait_h(6)
    step_z(11)
    unit(3, 0)
    step_z(12)
    wait_h(7)
    send_h(9)
    step_z(13)
    wait_core(2)
    wait_core(3)
    unit(0, 1)
    unit(2, 0)
    wait_h(8)
    finish(0)
    unit(1, 1)
    finish(1)
    unit(3, 1)
    finish(3)
    wait_h(9)
    unit(2, 1)
    finish(2)

    drain()
    for d in (1, 2, 3):
        ref = call.at[(y + d) % NY]
        remote(ref, ref, n_send.at[d], n_recv.at[d], at(x, y + d, z, c)).wait_recv()
    for n in range(1, NX * NY):
        ref = stats.at[n]
        remote(ref, ref, s_send.at[n], s_recv.at[n], at(x, y, z, c)).wait_recv()

    parts = [sbuf[x]] + [stats[n] for n in range(1, NX * NY)]
    tops = [p[0:4] for p in parts]
    top = tops[0]
    for t in tops[1:]:
        top = jnp.maximum(top, t)
    total = jnp.zeros((4, 128), jnp.float32)
    target = jnp.zeros((4, 128), jnp.float32)
    for p, t in zip(parts, tops):
        total = total + p[4:8] * jnp.exp(t - top)
        target = target + p[8:12]
    ce = top + jnp.log(total) - target
    ce_out[...] = ce

    ce = jnp.concatenate([ce[g : g + 1] for g in range(4)], axis=1)
    high = ce.astype(jnp.bfloat16).astype(jnp.float32)
    middle = (ce - high).astype(jnp.bfloat16).astype(jnp.float32)
    low = (ce - high) - middle
    which = lax.broadcasted_iota(jnp.int32, (16, ROWS), 0)
    pieces = jnp.where(which == 0, high, jnp.where(which == 1, middle, jnp.where(which == 2, low, 0.0)))
    pieces = pieces.astype(jnp.bfloat16)

    def means_of(rhs):
        sums = lax.dot_general(
            pieces, rhs, (((1,), (1,)), ((), ())), preferred_element_type=jnp.float32
        )
        return jnp.sum(sums, axis=0, keepdims=True) * (1.0 / 32768.0)

    means = means_of(call[...].reshape(128, ROWS))
    lanes = lax.broadcasted_iota(jnp.int32, (1, 128), 1)
    mine1[...] = jnp.where(lanes % 32 < RES, means, BIG)

    others = [(dx, dc) for dx in range(NX) for dc in range(NC) if (dx, dc) != (0, 0)]
    for dx, dc in others:
        n, m = dx * NC + dc, ((NX - dx) % NX) * NC + dc
        start(remote(mine1, rows1.at[m], g_send.at[n], g_recv.at[m], at(x + dx, y, z, c + dc)))
    mean_out[...] = means_of(call[y])[:, :RES]
    mine2[pl.ds(0, 1), :] = mine1[...]
    for dx, dc in others:
        n = dx * NC + dc
        ref = rows1.at[n]
        remote(ref, ref, g_send.at[n], g_recv.at[n], at(x + dx, y, z, c + dc)).wait_recv()
        mine2[pl.ds(n, 1), :] = rows1[n]
    for d in (4, 3, 5, 2, 6, 1, 7):
        m = NZ - d
        start(remote(mine2, rows2.at[m], k_send.at[d], k_recv.at[m], at(x, y, z + d, c)))
    rows2[0] = mine2[...]
    for d in (1, 7, 2, 6, 3, 5, 4):
        ref = rows2.at[d]
        remote(ref, ref, k_send.at[d], k_recv.at[d], at(x, y, z + d, c)).wait_recv()

    col = lax.broadcasted_iota(jnp.int32, (8, 128), 1)
    rowi = lax.broadcasted_iota(jnp.int32, (8, 128), 0)
    want = jnp.zeros((8, 128), jnp.float32)
    for q in range(8):
        want = jnp.where(rowi == q, ranks[q].astype(jnp.float32), want)

    def below(cands):
        counts = [jnp.zeros((8, 128), jnp.float32) for _ in cands]
        for n in range(NZ):
            for r in range(8):
                v = jnp.broadcast_to(rows2[n, pl.ds(r, 1), :], (8, 128))
                counts = [k + jnp.where(v < t, 1.0, 0.0) for k, t in zip(counts, cands)]
        return [jnp.broadcast_to(jnp.sum(k, axis=1, keepdims=True), (8, 128)) for k in counts]

    def pick(lo, cands):
        for k, t in zip(below(cands), cands):
            lo = jnp.where(k <= want, t, lo)
        return lo

    tiny = 2.0**-126
    lo = jnp.full((8, 128), tiny, jnp.float32)
    for e in (64, 16, 4, 1):
        first = lo * 2.0**e
        lo = pick(lo, [first, first * 2.0**e, first * 2.0**e * 2.0**e])
    unit0 = lo

    def refine(_, carry):
        lo, part = carry
        quarter = part * 0.25
        return pick(lo, [lo + quarter, lo + 2.0 * quarter, lo + 3.0 * quarter]), quarter

    lo, part = lax.fori_loop(0, 11, refine, (lo, unit0))
    lo = pick(lo, [lo + part * 0.5])
    none = below([jnp.full((8, 128), tiny, jnp.float32)])[0] > want
    lo = jnp.where(none, 0.0, lo)
    q_out[...] = jnp.sum(jnp.where(col == rowi, lo, 0.0), axis=0, keepdims=True)[:, :8]
    drain()


def emit(ce_in, mean_in, q_in, ce_out, mean_out, q_out, sem):
    copies = [
        pltpu.make_async_copy(src, dst, sem.at[i])
        for i, (src, dst) in enumerate(((ce_in, ce_out), (mean_in, mean_out), (q_in, q_out)))
    ]
    for copy in copies:
        copy.start()
    for copy in copies:
        copy.wait()


def shards(hidden, proj_weight, targets, counts, ranks):
    f32, bf16, i32 = jnp.float32, jnp.bfloat16, jnp.int32
    dma = pltpu.SemaphoreType.DMA
    hbm = pl.BlockSpec(memory_space=pl.ANY)
    vmem = pl.BlockSpec(memory_space=pltpu.VMEM)
    ce, means, quantiles = pl.pallas_call(
        kernel,
        out_shape=(
            jax.ShapeDtypeStruct((4, 128), f32),
            jax.ShapeDtypeStruct((1, RES), f32),
            jax.ShapeDtypeStruct((1, 8), f32),
        ),
        in_specs=[pl.BlockSpec(memory_space=pltpu.SMEM), hbm, hbm, hbm, hbm],
        out_specs=(vmem, vmem, vmem),
        scratch_shapes=[
            pltpu.VMEM((NX, NY, ROWS, KB), bf16),
            pltpu.VMEM((4, KB, WIDE), bf16),
            pltpu.VMEM((NX, ROWS, WIDE), f32),
            pltpu.VMEM((NX, ROWS, 128), f32),
            pltpu.VMEM((NX, 1, ROWS), i32),
            pltpu.VMEM((RES, 1, ROWS), i32),
            pltpu.VMEM((32, ROWS), f32),
            pltpu.VMEM((NY, 32, ROWS), bf16),
            pltpu.VMEM((NX, 16, 128), f32),
            pltpu.VMEM((NX * NY, 16, 128), f32),
            pltpu.VMEM((8, 1, 128), f32),
            pltpu.VMEM((1, 128), f32),
            pltpu.VMEM((NZ, 8, 128), f32),
            pltpu.VMEM((8, 128), f32),
            dma((2,)),
            dma((4,)), dma((4,)),
            dma((4,)), dma((4,)),
            dma((4, ITEMS)), dma((4, ITEMS)),
            dma((2, ZITEMS)), dma((2, ZITEMS)),
            dma((4 * NZ,)), dma((4 * NZ,)),
            dma((4,)), dma((4,)),
            dma((16,)), dma((16,)),
            dma((8,)), dma((8,)),
            dma((8,)), dma((8,)),
        ],
        compiler_params=pltpu.CompilerParams(
            collective_id=0, has_side_effects=True, vmem_limit_bytes=60 * 2**20
        ),
    )(ranks, hidden, proj_weight, targets.reshape(1, ROWS), counts.transpose(1, 0, 2))
    ce, means, quantiles = pl.pallas_call(
        emit,
        out_shape=(
            jax.ShapeDtypeStruct((ROWS,), f32),
            jax.ShapeDtypeStruct((1, RES), f32),
            jax.ShapeDtypeStruct((8,), f32),
        ),
        in_specs=[hbm, hbm, hbm],
        out_specs=(hbm, hbm, hbm),
        scratch_shapes=[dma((3,))],
    )(ce.reshape(ROWS), means, quantiles.reshape(8))
    return ce, means, quantiles


def solution(mesh):
    return jax.shard_map(
        shards,
        mesh=mesh,
        in_specs=(
            P("subset", "vocab"),
            P("subset", "vocab"),
            P("subset"),
            P("subset", "vocab", None),
            P(),
        ),
        out_specs=(P("subset"), P("subset", "vocab"), P()),
        check_vma=False,
    )
```
